32 devices in a mesh: grp: 2 (over x), patch: 16 (over z, y, core).
Axes of the slice: x: 2, y: 2, z: 4, core: 2. Of those that a mesh axis runs over, the one named last changes fastest.
Arguments:
- strength: float32 [3, 131072], P(None, ('grp', 'patch')), may hold values from -6 to 6
- fraction: float32 [3, 131072], P(None, ('grp', 'patch')), may hold values from 0 to 1
- cell: int32 [131072], P(('grp', 'patch')), may hold values from 0 to 38124
- patch_of: int32 [131072, 1], P(('grp', 'patch')), may hold values from 0 to 15; in each aligned block of 4096 rows (0 to 4095, 4096 to 8191, ...) at most 512 rows name the same one
- velocity: float32 [3, 128, 64, 256], P(None, 'patch', None, 'grp'), may hold values from -6 to 6
- body_mask: int32 [128, 64, 256], P('patch', None, 'grp'), may hold values 0 or 1
- stream_prev: float32 [3, 128, 64, 256], P(None, 'patch', None, 'grp'), may hold values from -2 to 2
Outputs:
- vorticity: float32 [3, 128, 64, 256], P(None, 'patch', None, 'grp')
- stream: float32 [3, 128, 64, 256], P(None, 'patch', None, 'grp')
The draws below stay inside these ranges and needn't reach their ends.
Inputs may be any that keep to these rules, and one draw needn't show every extreme that they name: `patch_of`: in each aligned block of 4096 rows (the rows of one device) no patch is named by more than 512 rows, a bound that some block reaches.
All inputs are finite; a program needn't handle non-finite values. No bound on the sum of `body_mask` on one device may be relied on, other than what follows from the above.
Results may differ from the reference program's by a relative error of at most 0.0018.
Values sent between devices are 32-bit elements; how exact they have to be, the bound alone decides.
A program may use at most 64 MiB of HBM per device.

```python
import math
import jax
import jax.numpy as jnp
import numpy as np
from jax import lax

P_DEV = 4096
TX = 8
TY = 64
TZ = 128
CAP = 512
PARTICLES = 131072
NX = 128
NZ = 256
INTERIOR = 38125
N_PATCH = 16


def touch_ends(result, key, low, top_value):
    shape = result.shape
    place = [jax.random.randint(jax.random.fold_in(key, axis), (), 0, shape[axis]) for axis in range(len(shape))]
    result = result.at[tuple(place)].set(low)
    longest = shape.index(max(shape))
    place[longest] = (place[longest] + 1) % shape[longest]
    return result.at[tuple(place)].set(top_value)


def block_levels(rng, shape, shards, smallest, high):
    loudness, own = 1.0, jax.random.fold_in(rng, 6)
    for position, parts in shards:
        draws = jnp.exp(jax.random.uniform(jax.random.fold_in(own, position), (parts,), jnp.float32, smallest / len(shards), high / len(shards)))
        loudness = loudness * jnp.repeat(draws, shape[position] // parts).reshape([-1 if axis == position else 1 for axis in range(len(shape))])
    return loudness


def assign_block(stream_key, own, number, rows, count, top, most, slope):
    ranking = jax.random.permutation(stream_key, count)
    crowded, usual = shares(count, rows * top, most, slope, True), shares(count, rows * top, most, slope, False)
    places = jnp.arange(count)

    def named(tallies, turn):
        used = int((tallies > 0).sum())
        fixed = max(1, used // 4)
        passed = fixed + (places - fixed + turn * (used - fixed)) % max(1, count - fixed)
        return jnp.zeros((count,), jnp.int32).at[ranking[jnp.where(places < fixed, places, passed)]].set(jnp.asarray(tallies, jnp.int32))

    tallies = jnp.where(number % 4 == 0, named(crowded, number // 4), named(usual, number - number // 4 - 1))
    mixed = jax.random.permutation(jax.random.fold_in(own, 3), count)
    donor, sink = mixed[0:count // 2 * 2:2], mixed[1:count // 2 * 2:2]
    room = jnp.minimum(tallies[donor] - 1, most - tallies[sink]) // 2
    room = jnp.where((donor == ranking[0]) | (sink == ranking[0]) | (tallies[sink] == 0), 0, jnp.maximum(room, 0))
    passed = jax.random.randint(jax.random.fold_in(own, 4), (count // 2,), 0, 1 << 20) % (room + 1)
    tallies = tallies.at[donor].add(-passed).at[sink].add(passed)
    items = jnp.searchsorted(jnp.cumsum(tallies), jnp.arange(rows * top), side="right").astype(jnp.int32)
    grid = items.reshape(top, rows).T
    grid = grid[jax.random.permutation(jax.random.fold_in(own, 1), rows)]
    turn = jax.random.randint(jax.random.fold_in(own, 2), (rows, 1), 0, top)
    return jnp.take_along_axis(grid, (jnp.arange(top)[None, :] + turn) % top, axis=1)


def shares(count, total, reach, lean, full):
    weights = [(1 << 20) // math.isqrt(standing ** lean) + 1 for standing in range(1, count + 1)]
    largest = reach if full else min(reach, max(-(-total // count), total * weights[0] // sum(weights)))
    least = 1 if total - largest >= count - 1 else 0
    counts, surplus = [largest] + [least] * (count - 1), total - largest - least * (count - 1)
    while surplus > 0:
        free = [i for i in range(1, count) if counts[i] < largest] or [i for i in range(1, count) if counts[i] < reach]
        whole, remaining = sum([weights[i] for i in free]), surplus
        for i in free:
            extra = min(reach - counts[i], max(1, remaining * weights[i] // whole), surplus)
            counts[i] = counts[i] + extra
            surplus = surplus - extra
    return np.array(counts)


def scatter_about(key, dims, spread, reach, shards=(), kind=jnp.bfloat16):
    entries = jax.random.normal(key, dims, jnp.float32) * spread
    if len(shards) > 0:
        entries = block_levels(key, dims, shards, -0.22, 0.18) * entries
    return jnp.clip(entries, min=-reach, max=reach).astype(kind)


def setup_inputs(seed: int = 0) -> dict:
    seeds = jax.random.split(jax.random.key(seed), 8)
    strength = scatter_about(seeds[0], (3, PARTICLES), 1.0, 6.0, ((1, 32),), jnp.float32)
    fraction = jnp.clip(1.0 * jax.random.uniform(seeds[1], (3, PARTICLES), jnp.float32) ** block_levels(seeds[1], (3, PARTICLES), ((1, 32),), -0.2, 0.2), 0.0, 1.0)
    cell = touch_ends(jax.random.randint(seeds[2], (PARTICLES,), 0, INTERIOR), jax.random.fold_in(seeds[2], 1), 0, INTERIOR - 1).astype(jnp.int32)
    patch_of_keys = jax.random.split(jax.random.fold_in(seeds[3], 1), PARTICLES // P_DEV)
    patch_of_turns = jax.random.permutation(jax.random.fold_in(seeds[3], 3), PARTICLES // P_DEV)
    patch_of = jax.vmap(lambda own, number: assign_block(jax.random.fold_in(seeds[3], 2), own, number, P_DEV, N_PATCH, 1, CAP, 2))(patch_of_keys, patch_of_turns).reshape((PARTICLES, 1))
    velocity = scatter_about(seeds[4], (3, NX, TY, NZ), 1.0, 6.0, ((1, 16), (3, 2)), jnp.float32)
    body_mask = touch_ends((jax.random.randint(seeds[5], (NX, TY, NZ), 0, 3) < 1).astype(jnp.int32), jax.random.fold_in(seeds[5], 1), 0, 1)
    stream_prev = scatter_about(seeds[6], (3, NX, TY, NZ), 0.3, 2.0, ((1, 16), (3, 2)), jnp.float32)
    return {"strength": strength, "fraction": fraction, "cell": cell, "patch_of": patch_of, "velocity": velocity, "body_mask": body_mask, "stream_prev": stream_prev}


DT_STEP = 0.5
PEN_GAIN = 0.8


def kernel(distance):
    distance = jnp.abs(distance)
    near_part = 1.0 - 2.5 * distance * distance + 1.5 * distance * distance * distance
    far_part = 0.5 * (2.0 - distance) * (2.0 - distance) * (1.0 - distance)
    return jnp.where(distance < 1.0, near_part, jnp.where(distance < 2.0, far_part, 0.0 * distance))


def shifted(extended, along, amount):
    cutting = [slice(None)]
    for extent in extended.shape[1:]:
        cutting.append(slice(1, extent - 1))
    cutting[along] = slice(amount, extended.shape[along] - 2 + amount)
    return extended[tuple(cutting)]


def differ(extended, along):
    return (shifted(extended, along, 2) - shifted(extended, along, 0)) * 0.5


def neighbours(extended):
    summed = shifted(extended, 1, 2) + shifted(extended, 1, 0)
    summed = summed + shifted(extended, 2, 2) + shifted(extended, 2, 0)
    summed = summed + shifted(extended, 3, 2) + shifted(extended, 3, 0)
    return summed


def source_terms(deposited, extended):
    speed = extended[:3]
    penal = extended[3:]
    grad_speed = [differ(speed, 1), differ(speed, 2), differ(speed, 3)]
    stretch = deposited[0:1] * grad_speed[0] + deposited[1:2] * grad_speed[1] + deposited[2:3] * grad_speed[2]
    grad_penal = [differ(penal, 1), differ(penal, 2), differ(penal, 3)]
    curl_penal = jnp.stack([grad_penal[1][2] - grad_penal[2][1], grad_penal[2][0] - grad_penal[0][2], grad_penal[0][1] - grad_penal[1][0]])
    return deposited + DT_STEP * stretch + curl_penal


def reference(strength, fraction, cell, patch_of, velocity, body_mask, stream_prev):
    span_y = TY - 3
    span_z = TZ - 3
    rows_all = jnp.arange(PARTICLES, dtype=jnp.int32)
    group_of = (rows_all // (P_DEV * N_PATCH)).astype(jnp.int32)
    target = patch_of[:, 0].astype(jnp.int32)
    cells = cell.astype(jnp.int32)
    base_x = (cells // (span_y * span_z) + 1 + target * TX).astype(jnp.int32)
    base_y = ((cells // span_z) % span_y + 1).astype(jnp.int32)
    base_z = (cells % span_z + 1 + group_of * TZ).astype(jnp.int32)
    offsets = (jnp.arange(4, dtype=jnp.int32) - 1).astype(jnp.int32)
    block_size = math.gcd(PARTICLES, 65536)
    block_count = PARTICLES // block_size

    def accumulate(turn, grid_flat):
        first_row = (turn * block_size).astype(jnp.int32)
        part_strength = lax.dynamic_slice_in_dim(strength, first_row, block_size, 1)
        part_fraction = lax.dynamic_slice_in_dim(fraction, first_row, block_size, 1)
        row_x = lax.dynamic_slice_in_dim(base_x, first_row, block_size, 0)
        row_y = lax.dynamic_slice_in_dim(base_y, first_row, block_size, 0)
        row_z = lax.dynamic_slice_in_dim(base_z, first_row, block_size, 0)
        weight_x = kernel(offsets[:, None].astype(jnp.float32) - part_fraction[0][None, :])
        weight_y = kernel(offsets[:, None].astype(jnp.float32) - part_fraction[1][None, :])
        weight_z = kernel(offsets[:, None].astype(jnp.float32) - part_fraction[2][None, :])
        factor = (part_strength[:, None, None, :] * weight_x[None, :, None, :]) * weight_y[None, None, :, :]
        factor = lax.optimization_barrier(factor.astype(jnp.bfloat16)).astype(jnp.float32)
        weight_low = lax.optimization_barrier(weight_z.astype(jnp.bfloat16)).astype(jnp.float32)
        values = factor[:, :, :, None, :] * weight_low[None, None, None, :, :]
        glob_x = (row_x[None, :] + offsets[:, None]).astype(jnp.int32)
        glob_y = (row_y[None, :] + offsets[:, None]).astype(jnp.int32)
        glob_z = (row_z[None, :] + offsets[:, None]).astype(jnp.int32)
        flat_index = ((glob_x[:, None, None, :] * TY + glob_y[None, :, None, :]) * NZ + glob_z[None, None, :, :]).astype(jnp.int32)
        return grid_flat.at[:, flat_index.reshape(-1)].add(values.reshape(3, -1))

    grid_flat = jnp.zeros((3, NX * TY * NZ), jnp.float32)
    grid_flat = lax.fori_loop(0, block_count, accumulate, grid_flat)
    deposited = grid_flat.reshape(3, NX, TY, NZ)
    penal = -PEN_GAIN * body_mask.astype(jnp.float32)[None] * velocity
    stacked = jnp.concatenate([velocity, penal], axis=0)
    extended = jnp.pad(stacked, ((0, 0), (1, 1), (1, 1), (1, 1)))
    vorticity = source_terms(deposited, extended)
    stream = stream_prev
    for sweep_turn in range(2):
        padded = jnp.pad(stream, ((0, 0), (1, 1), (1, 1), (1, 1)))
        stream = (neighbours(padded) + vorticity) / 6.0
    return vorticity, stream
```

```python
import jax
import jax.numpy as jnp
from jax import lax
from jax.experimental import pallas as pl
from jax.experimental.pallas import tpu as pltpu
from jax.sharding import PartitionSpec as P

DT_STEP = 0.5
PEN_GAIN = 0.8
ROWS = 8
VMEM = pl.BlockSpec(memory_space=pltpu.VMEM)
MESH = pl.DeviceIdType.MESH
NT = (((1,), (1,)), ((), ()))


def kernel(distance):
    d = jnp.minimum(jnp.abs(distance), 2.0)
    near_part = 1.0 + d * d * (1.5 * d - 2.5)
    t = 2.0 - d
    return jnp.where(d < 1.0, near_part, 0.5 * t * t * (1.0 - d))


def iota(shape, dim):
    return lax.broadcasted_iota(jnp.int32, shape, dim)


def pack_column(plane, lane, high, packed):
    width = plane.shape[1]
    turn = (lane + 1) % width if high else lane
    moved = pltpu.roll(plane, turn, 1) if turn else plane
    return jnp.where(iota(plane.shape, 1) == lane, moved, packed)


def along_z(plane, low, high, lane):
    width = plane.shape[1]
    at = iota(plane.shape, 1)
    from_low = pltpu.roll(low, (width - lane) % width, 1) if lane else low
    turn = width - 1 - lane
    from_high = pltpu.roll(high, turn, 1) if turn else high
    below = jnp.where(at == 0, from_low, pltpu.roll(plane, 1, 1))
    above = jnp.where(at == width - 1, from_high, pltpu.roll(plane, width - 1, 1))
    return below, above


def along_y(plane):
    height = plane.shape[0]
    at = iota(plane.shape, 0)
    below = jnp.where(at == 0, 0.0, pltpu.roll(plane, 1, 0))
    above = jnp.where(at == height - 1, 0.0, pltpu.roll(plane, height - 1, 0))
    return below, above


def route(strength, fraction, cell, target, out, amid):
    rows = strength.shape[1]
    patches, _, capacity = out.shape
    chunk = min(512, rows)
    tri = (iota((chunk, chunk), 0) < iota((chunk, chunk), 1)).astype(jnp.float32).astype(jnp.bfloat16)
    running = jnp.zeros((patches, 1), jnp.float32)
    for turn in range(rows // chunk):
        if turn == min(3, rows // chunk - 1):
            amid()
        at = pl.ds(turn * chunk, chunk)
        named = target[:, at]
        chosen = (iota((patches, chunk), 0) == named).astype(jnp.float32)
        prefix = jnp.dot(chosen.astype(jnp.bfloat16), tri, preferred_element_type=jnp.float32) + running
        running = running + jnp.sum(chosen, axis=1, keepdims=True)
        within = jnp.sum(prefix * chosen, axis=0, keepdims=True).astype(jnp.int32)
        slots = (iota((capacity, chunk), 0) == within).astype(jnp.float32).astype(jnp.bfloat16)
        value = jnp.concatenate(
            [strength[:, at], fraction[:, at], cell[:, at].astype(jnp.float32), jnp.zeros((1, chunk), jnp.float32)],
            axis=0,
        )
        pieces = []
        for part in range(3):
            piece = value.astype(jnp.bfloat16).astype(jnp.float32)
            value = value - piece
            pieces.extend(jnp.where(named == p, piece, 0.0) for p in range(patches))
        left = jnp.concatenate(pieces, axis=0).astype(jnp.bfloat16)
        product = lax.dot_general(left, slots, NT, preferred_element_type=jnp.float32)
        size = patches * ROWS
        moved = (product[:size] + product[size : 2 * size]) + product[2 * size :]
        moved = moved.reshape(patches, ROWS, capacity)
        if turn == 0:
            out[...] = moved
        else:
            out[...] += moved


def pack_faces(velocity, mask, stream, out):
    count_x = velocity.shape[1] - 2
    low = high = jnp.zeros(out.shape[1:], jnp.float32)
    for k in range(3):
        for x in range(count_x):
            speed = velocity[k, x + 1]
            penal = -PEN_GAIN * mask[x + 1].astype(jnp.float32) * speed
            for part, plane in enumerate((speed, penal, stream[k, x + 1])):
                lane = (part * 3 + k) * count_x + x
                low = pack_column(plane, lane, False, low)
                high = pack_column(plane, lane, True, high)
    out[0] = low
    out[1] = high


def deposit_slots(data, total, shape):
    count_x, count_y, count_z = shape
    span_y, span_z = count_y - 3, count_z - 3
    slots = data.shape[1]
    cell = data[6:7]
    quot_x = ((cell + 0.5) * (1.0 / (span_y * span_z))).astype(jnp.int32).astype(jnp.float32)
    rest = cell - quot_x * (span_y * span_z)
    quot_y = ((rest + 0.5) * (1.0 / span_z)).astype(jnp.int32).astype(jnp.float32)
    quot_z = rest - quot_y * span_z

    def weights(count, quot, part):
        offsets = (iota((8, slots), 0) - 1).astype(jnp.float32)
        value = kernel(offsets - part)
        away = iota((count, slots), 0) - quot.astype(jnp.int32)
        result = jnp.where(away == 3, value[3:4], 0.0)
        for o in range(3):
            result = jnp.where(away == o, value[o : o + 1], result)
        return result

    weight_x = weights(count_x, quot_x, data[3:4])
    weight_y = weights(count_y, quot_y, data[4:5])
    weight_z = weights(count_z, quot_z, data[5:6]).astype(jnp.bfloat16)
    for k in range(3):
        scaled = data[k : k + 1] * weight_x
        factor = jnp.concatenate(
            [(scaled[x : x + 1] * weight_y).astype(jnp.bfloat16) for x in range(count_x)], axis=0
        )
        size = count_x * count_y
        total[k * size : (k + 1) * size] += lax.dot_general(
            factor, weight_z, NT, preferred_element_type=jnp.float32
        )


def swirl(total, velocity, mask, z_low, z_high, vorticity):
    _, count_x, count_y, _ = vorticity.shape
    low, high = z_low[...], z_high[...]
    for x in range(count_x):
        before, own, after = [-PEN_GAIN * mask[x + i].astype(jnp.float32) for i in range(3)]
        moved = [total[(k * count_x + x) * count_y : (k * count_x + x + 1) * count_y] for k in range(3)]
        curl = [moved[k] for k in range(3)]
        for k in range(3):
            under, plane, over = [velocity[k, x + i] for i in range(3)]
            y_below, y_above = along_y(plane)
            lane = k * count_x + x
            z_below, z_above = along_z(plane, low, high, lane)
            stretch = moved[0] * (over - under) + moved[1] * (y_above - y_below) + moved[2] * (z_above - z_below)
            curl[k] = curl[k] + (0.5 * DT_STEP) * stretch
            penal = own * plane
            if k != 0:
                change = 0.5 * (after * over - before * under)
                curl[3 - k] = curl[3 - k] + (change if k == 1 else -change)
            if k != 1:
                y_below, y_above = along_y(penal)
                change = 0.5 * (y_above - y_below)
                curl[2 - k] = curl[2 - k] + (change if k == 2 else -change)
            if k != 2:
                z_below, z_above = along_z(penal, low, high, 3 * count_x + lane)
                change = 0.5 * (z_above - z_below)
                curl[1 - k] = curl[1 - k] + (change if k == 0 else -change)
        for k in range(3):
            vorticity[k, x] = curl[k]


def within_plane(plane, low, high, lane):
    y_below, y_above = along_y(plane)
    z_below, z_above = along_z(plane, low, high, lane)
    return y_below + y_above + z_below + z_above


def first_sweep(stream, vorticity, low, high, first_lane, middle):
    _, count_x, _, _ = vorticity.shape
    for x in [0, count_x - 1] + list(range(1, count_x - 1)):
        for k in range(3):
            lane = first_lane + k * count_x + x
            summed = stream[k, x] + stream[k, x + 2] + within_plane(stream[k, x + 1], low, high, lane)
            middle[k, x + 1] = (summed + vorticity[k, x]) * (1.0 / 6.0)


def second_sweep(middle, vorticity, result):
    _, count_x, count_y, count_z = vorticity.shape
    empty = jnp.zeros((count_y, count_z), jnp.float32)
    for k in range(3):
        for x in range(count_x):
            summed = within_plane(middle[k, x + 1], empty, empty, 0)
            if x > 0:
                summed = summed + middle[k, x]
            if x < count_x - 1:
                summed = summed + middle[k, x + 2]
            result[k, x] = (summed + vorticity[k, x]) * (1.0 / 6.0)


def add_faces(middle, low, high, result):
    _, count_x, count_y, count_z = result.shape
    at = iota((count_y, count_z), 1)
    for k in range(3):
        for x in range(count_x):
            lane = k * count_x + x
            from_low = pltpu.roll(low, (count_z - lane) % count_z, 1) if lane else low
            from_high = pltpu.roll(high, count_z - 1 - lane, 1)
            extra = jnp.where(at == 0, from_low, 0.0) + jnp.where(at == count_z - 1, from_high, 0.0)
            if x == 0:
                extra = extra + middle[k, 0]
            if x == count_x - 1:
                extra = extra + middle[k, count_x + 1]
            result[k, x] += extra * (1.0 / 6.0)


def pack_stream(stream, low_ref, high_ref):
    count_x = stream.shape[1] - 2
    low = high = jnp.zeros(low_ref.shape, jnp.float32)
    for k in range(3):
        for x in range(count_x):
            low = pack_column(stream[k, x + 1], k * count_x + x, False, low)
            high = pack_column(stream[k, x + 1], k * count_x + x, True, high)
    low_ref[...] = low
    high_ref[...] = high


def step(
    strength_in, fraction_in, cell_in, target_in, velocity_in, mask_in, stream_in,
    vorticity, result, strength, fraction, cell, target, velocity, mask, stream,
    outgoing, arrived, total, middle, z_out, z_in, m_out, m_in,
    fetch_sem, send_sem, recv_sem, face_send, face_recv, z_send, z_recv, mx_send, mx_recv, mz_send, mz_recv,
):
    groups, patches = lax.axis_size("grp"), lax.axis_size("patch")
    g, p = lax.axis_index("grp"), lax.axis_index("patch")
    count_x = vorticity.shape[1]
    fetches = [
        (strength_in, strength), (fraction_in, fraction), (cell_in, cell), (target_in, target),
        (velocity_in, velocity.at[:, pl.ds(1, count_x)]),
        (mask_in, mask.at[pl.ds(1, count_x)]),
        (stream_in, stream.at[:, pl.ds(1, count_x)]),
    ]
    fetches = [pltpu.make_async_copy(a, b, fetch_sem.at[i]) for i, (a, b) in enumerate(fetches)]
    for fetch in fetches:
        fetch.start()

    barrier = pltpu.get_barrier_semaphore()

    def greet(i, carry):
        pl.semaphore_signal(barrier, inc=1, device_id={"patch": lax.rem(p + i, patches)}, device_id_type=MESH)
        return carry

    lax.fori_loop(1, patches, greet, 0)
    sides = (
        (0, "patch", p, p > 0, p - 1), (1, "patch", p, p < patches - 1, p + 1),
        (0, "grp", g, g > 0, g - 1), (1, "grp", g, g < groups - 1, g + 1),
    )
    x_sides = [(side, there, {axis: who}) for side, axis, _, there, who in sides[:2]]
    z_sides = [(side, there, {axis: who}) for side, axis, _, there, who in sides[2:]]
    for side, there, who in z_sides:
        @pl.when(there)
        def _():
            pl.semaphore_signal(barrier, inc=1, device_id=who, device_id_type=MESH)

    for fetch in fetches[:4]:
        fetch.wait()
    for side, there, who in x_sides:
        @pl.when(jnp.logical_not(there))
        def _():
            rim = side * (count_x + 1)
            empty = jnp.zeros(velocity.shape[2:], jnp.float32)
            mask[rim] = jnp.zeros(velocity.shape[2:], jnp.int32)
            for k in range(3):
                velocity[k, rim] = empty
                stream[k, rim] = empty
                middle[k, rim] = empty
    for side, there, who in z_sides:
        @pl.when(jnp.logical_not(there))
        def _():
            z_in[side] = jnp.zeros(z_in.shape[1:], jnp.float32)
            m_in[side] = jnp.zeros(m_in.shape[1:], jnp.float32)

    def remote(a, b, send, recv, who):
        return pltpu.make_async_remote_copy(
            src_ref=a, dst_ref=b, send_sem=send, recv_sem=recv, device_id=who, device_id_type=MESH
        )

    def faces(side, who):
        own, rim = 1 + side * (count_x - 1), (1 - side) * (count_x + 1)
        return [
            remote(a, b, face_send.at[side, i], face_recv.at[1 - side, i], who)
            for i, (a, b) in enumerate((
                (velocity.at[:, own], velocity.at[:, rim]),
                (mask.at[own], mask.at[rim]),
                (stream.at[:, own], stream.at[:, rim]),
            ))
        ]

    def z_face(side, who):
        return [remote(z_out.at[side], z_in.at[1 - side], z_send.at[side], z_recv.at[1 - side], who)]

    def m_face(side, who):
        own, rim = 1 + side * (count_x - 1), (1 - side) * (count_x + 1)
        return [remote(middle.at[:, own], middle.at[:, rim], mx_send.at[side], mx_recv.at[1 - side], who)]

    def mz_face(side, who):
        return [remote(m_out.at[side], m_in.at[1 - side], mz_send.at[side], mz_recv.at[1 - side], who)]

    def start(make, ways):
        for side, there, who in ways:
            @pl.when(there)
            def _():
                for copy in make(side, who):
                    copy.start()

    def finish(make, ways, sent):
        for side, there, who in ways:
            @pl.when(there)
            def _():
                for copy in make(side if sent else 1 - side, who):
                    if sent:
                        copy.wait_send()
                    else:
                        copy.wait_recv()

    def send_faces():
        for fetch in fetches[4:]:
            fetch.wait()
        pack_faces(velocity, mask, stream, z_out)
        pl.semaphore_wait(barrier, patches - 1 + (g > 0).astype(jnp.int32) + (g < groups - 1).astype(jnp.int32))
        start(faces, x_sides)
        start(z_face, z_sides)

    route(strength, fraction, cell, target, outgoing, send_faces)

    def slots(i):
        other = lax.rem(p + i, patches)
        return remote(outgoing.at[other, pl.ds(0, 7)], arrived.at[i, pl.ds(0, 7)], send_sem.at[i], recv_sem.at[i], {"patch": other})

    def send(i, carry):
        slots(i).start()
        return carry

    lax.fori_loop(1, patches, send, 0)
    total[...] = jnp.zeros_like(total)
    deposit_slots(outgoing[p], total, vorticity.shape[1:])

    def take(i, carry):
        slots(i).wait_recv()
        deposit_slots(arrived[i], total, vorticity.shape[1:])
        return carry

    lax.fori_loop(1, patches, take, 0)
    finish(faces, x_sides, False)
    finish(z_face, z_sides, False)
    swirl(total, velocity, mask, z_in.at[0], z_in.at[1], vorticity)
    first_sweep(stream, vorticity, z_in[0], z_in[1], 6 * count_x, middle)
    pack_stream(middle, m_out.at[0], m_out.at[1])
    start(m_face, x_sides)
    start(mz_face, z_sides)
    second_sweep(middle, vorticity, result)
    finish(m_face, x_sides, False)
    finish(mz_face, z_sides, False)
    add_faces(middle, m_in[0], m_in[1], result)

    def sent(i, carry):
        slots(i).wait_send()
        return carry

    lax.fori_loop(1, patches, sent, 0)
    finish(faces, x_sides, True)
    finish(z_face, z_sides, True)
    finish(m_face, x_sides, True)
    finish(mz_face, z_sides, True)


def write_out(a, b, c, d, sem):
    x = pltpu.make_async_copy(a, c, sem.at[0])
    y = pltpu.make_async_copy(b, d, sem.at[1])
    x.start()
    y.start()
    x.wait()
    y.wait()


def shards(strength, fraction, cell, patch_of, velocity, body_mask, stream_prev):
    rows = patch_of.shape[0]
    patches = lax.axis_size("patch")
    capacity = 2 * rows // patches
    parts, count_x, count_y, count_z = velocity.shape
    plane = (count_y, count_z)
    room = lambda *shape: pltpu.VMEM(shape, jnp.float32)
    ints = lambda *shape: pltpu.VMEM(shape, jnp.int32)
    dma = lambda *shape: pltpu.SemaphoreType.DMA(shape)
    vorticity, stream = pl.pallas_call(
        step,
        out_shape=[pltpu.VMEM(velocity.shape, jnp.float32)] * 2,
        in_specs=[pl.BlockSpec(memory_space=pltpu.HBM)] * 7,
        out_specs=[VMEM] * 2,
        scratch_shapes=[
            room(3, rows), room(3, rows), ints(1, rows), ints(1, rows),
            room(parts, count_x + 2, *plane), ints(count_x + 2, *plane), room(parts, count_x + 2, *plane),
            room(patches, ROWS, capacity), room(patches, ROWS, capacity),
            room(parts * count_x * count_y, count_z), room(parts, count_x + 2, *plane),
            room(2, *plane), room(2, *plane), room(2, *plane), room(2, *plane),
            dma(9), dma(patches), dma(patches), dma(2, 3), dma(2, 3),
            dma(2), dma(2), dma(2), dma(2), dma(2), dma(2),
        ],
        compiler_params=pltpu.CompilerParams(
            collective_id=0, has_side_effects=True, vmem_limit_bytes=50*2**20
        ),
    )(*[pltpu.with_memory_space_constraint(a, pltpu.HBM) for a in (strength, fraction, cell.reshape(1, rows), patch_of.reshape(1, rows), velocity, body_mask, stream_prev)])
    vorticity, stream = pl.pallas_call(
        write_out,
        out_shape=[jax.ShapeDtypeStruct(velocity.shape, jnp.float32)] * 2,
        in_specs=[VMEM] * 2,
        out_specs=[pl.BlockSpec(memory_space=pltpu.HBM)] * 2,
        scratch_shapes=[dma(2)],
    )(pltpu.with_memory_space_constraint(vorticity, pltpu.VMEM), pltpu.with_memory_space_constraint(stream, pltpu.VMEM))
    return (vorticity, stream)


def solution(mesh):
    in_specs = (
        P(None, ("grp", "patch")),
        P(None, ("grp", "patch")),
        P(("grp", "patch")),
        P(("grp", "patch"), None),
        P(None, "patch", None, "grp"),
        P("patch", None, "grp"),
        P(None, "patch", None, "grp"),
    )
    out_specs = (P(None, "patch", None, "grp"), P(None, "patch", None, "grp"))
    return jax.shard_map(shards, mesh=mesh, in_specs=in_specs, out_specs=out_specs, check_vma=False)
```

```python
import jax
import jax.numpy as jnp
from jax import lax
from jax.experimental import pallas as pl
from jax.experimental.pallas import tpu as pltpu
from jax.sharding import PartitionSpec as P

DT_STEP = 0.5
PEN_GAIN = 0.8
ROWS = 8
HBM = pl.BlockSpec(memory_space=pltpu.HBM)
VMEM = pl.BlockSpec(memory_space=pltpu.VMEM)
MESH = pl.DeviceIdType.MESH
NT = (((1,), (1,)), ((), ()))


def kernel(distance):
    d = jnp.minimum(jnp.abs(distance), 2.0)
    near_part = 1.0 + d * d * (1.5 * d - 2.5)
    t = 2.0 - d
    return jnp.where(d < 1.0, near_part, 0.5 * t * t * (1.0 - d))


def iota(shape, dim):
    return lax.broadcasted_iota(jnp.int32, shape, dim)


def pack_column(plane, lane, high, packed):
    width = plane.shape[1]
    turn = (lane + 1) % width if high else lane
    moved = pltpu.roll(plane, turn, 1) if turn else plane
    return jnp.where(iota(plane.shape, 1) == lane, moved, packed)


def along_z(plane, low, high, lane):
    width = plane.shape[1]
    at = iota(plane.shape, 1)
    from_low = pltpu.roll(low, (width - lane) % width, 1) if lane else low
    turn = width - 1 - lane
    from_high = pltpu.roll(high, turn, 1) if turn else high
    below = jnp.where(at == 0, from_low, pltpu.roll(plane, 1, 1))
    above = jnp.where(at == width - 1, from_high, pltpu.roll(plane, width - 1, 1))
    return below, above


def along_y(plane):
    height = plane.shape[0]
    at = iota(plane.shape, 0)
    below = jnp.where(at == 0, 0.0, pltpu.roll(plane, 1, 0))
    above = jnp.where(at == height - 1, 0.0, pltpu.roll(plane, height - 1, 0))
    return below, above


def rank(target, patches, chunk):
    turns = target.shape[1] // chunk
    tri = (iota((chunk, chunk), 0) < iota((chunk, chunk), 1)).astype(jnp.float32).astype(jnp.bfloat16)
    chosen = [
        (iota((patches, chunk), 0) == target[:, pl.ds(turn * chunk, chunk)]).astype(jnp.float32) for turn in range(turns)
    ]
    stacked = jnp.concatenate(chosen, axis=0).astype(jnp.bfloat16)
    prefix = jnp.dot(stacked, tri, preferred_element_type=jnp.float32)
    running = jnp.zeros((patches, 1), jnp.float32)
    result = []
    for turn in range(turns):
        named = chosen[turn]
        before = prefix[turn * patches : (turn + 1) * patches] + running
        running = running + jnp.sum(named, axis=1, keepdims=True)
        result.append(jnp.sum(before * named, axis=0, keepdims=True).astype(jnp.int32))
    return result


def route(strength, fraction, cell, target, out, amid):
    rows = strength.shape[1]
    patches, _, capacity = out.shape
    chunk = min(512, rows)
    turns = rows // chunk
    places = rank(target, patches, chunk)
    for turn in range(turns):
        if turn == turns // 2:
            amid()
        at = pl.ds(turn * chunk, chunk)
        named = target[:, at]
        slots = (iota((capacity, chunk), 0) == places[turn]).astype(jnp.float32).astype(jnp.bfloat16)
        value = jnp.concatenate(
            [strength[:, at], fraction[:, at], cell[:, at].astype(jnp.float32), jnp.zeros((1, chunk), jnp.float32)],
            axis=0,
        )
        coarse = value.astype(jnp.bfloat16).astype(jnp.float32)
        fine = value - coarse
        pieces = []
        for p in range(patches):
            hit = named == p
            pieces.extend((jnp.where(hit, coarse, 0.0), jnp.where(hit, fine, 0.0)))
        left = jnp.concatenate(pieces, axis=0).astype(jnp.bfloat16)
        product = lax.dot_general(left, slots, NT, preferred_element_type=jnp.float32)
        product = product.reshape(patches, 2 * ROWS, capacity)
        moved = product[:, :ROWS] + product[:, ROWS:]
        if turn == 0:
            out[...] = moved
        else:
            out[...] += moved


def pack_faces(velocity, mask, stream, out):
    count_x = velocity.shape[1] - 2
    low = high = jnp.zeros(out.shape[1:], jnp.float32)
    for k in range(3):
        for x in range(count_x):
            speed = velocity[k, x + 1]
            penal = -PEN_GAIN * mask[x + 1].astype(jnp.float32) * speed
            for part, plane in enumerate((speed, penal, stream[k, x + 1])):
                lane = (part * 3 + k) * count_x + x
                low = pack_column(plane, lane, False, low)
                high = pack_column(plane, lane, True, high)
    out[0] = low
    out[1] = high


def spread(pattern, group, count):
    low, high = pattern[:ROWS], pattern[ROWS:]
    hits = [group == at for at in range(count)]
    result = []
    for at in range(count):
        piece = jnp.where(hits[at], low, 0.0)
        result.append(jnp.where(hits[at - 1], high, piece) if at else piece)
    return result


def deposit_operands(data, shape):
    count_x, count_y, count_z = shape
    span_y, span_z = count_y - 3, count_z - 3
    half = count_y // 2
    slots = data.shape[1]
    cell = data[6:7]
    quot_x = ((cell + 0.5) * (1.0 / (span_y * span_z))).astype(jnp.int32).astype(jnp.float32)
    rest = cell - quot_x * (span_y * span_z)
    quot_y = ((rest + 0.5) * (1.0 / span_z)).astype(jnp.int32)
    quot_z = (rest - quot_y.astype(jnp.float32) * span_z).astype(jnp.int32)
    upper = quot_y >= half
    quot_y = jnp.where(upper, quot_y - half, quot_y)

    def pattern(quot, part):
        group = lax.shift_right_logical(quot, 3)
        first = (quot - group * ROWS).astype(jnp.float32) + 1.0
        away = iota((2 * ROWS, slots), 0).astype(jnp.float32) - first
        return group, kernel(away - part)

    weight_x = kernel((iota((count_x, slots), 0).astype(jnp.float32) - (quot_x + 1.0)) - data[3:4])
    group_y, weight_y = pattern(quot_y, data[4:5])
    group_z, weight_z = pattern(quot_z, data[5:6])
    window = spread(weight_y, group_y, half // ROWS + 1)
    depth = jnp.concatenate(spread(weight_z, group_z, count_z // ROWS), axis=0)
    depth = jnp.concatenate([jnp.where(upper, 0.0, depth), jnp.where(upper, depth, 0.0)], axis=0).astype(jnp.bfloat16)
    pieces = []
    for k in range(3):
        scaled = data[k : k + 1] * weight_x
        for x in range(count_x):
            line = scaled[x : x + 1]
            pieces.extend(line * piece for piece in window)
    return jnp.concatenate(pieces, axis=0).astype(jnp.bfloat16), depth


def deposit(blocks, total, shape):
    pairs = [deposit_operands(block, shape) for block in blocks]
    left = jnp.concatenate([pair[0] for pair in pairs], axis=1)
    right = jnp.concatenate([pair[1] for pair in pairs], axis=1)
    total[...] += lax.dot_general(left, right, NT, preferred_element_type=jnp.float32)


def prepare(velocity, mask, stream, z_low, z_high, slope, curl, middle):
    _, count_x, count_y, _ = curl.shape
    low, high = z_low[...], z_high[...]
    for x in range(count_x):
        before, own, after = [-PEN_GAIN * mask[x + i].astype(jnp.float32) for i in range(3)]
        turned = [None] * 3

        def add(k, change):
            turned[k] = change if turned[k] is None else turned[k] + change

        for k in range(3):
            under, plane, over = [velocity[k, x + i] for i in range(3)]
            y_below, y_above = along_y(plane)
            lane = k * count_x + x
            z_below, z_above = along_z(plane, low, high, lane)
            slope[0, k, x] = (0.5 * DT_STEP) * (over - under)
            slope[1, k, x] = (0.5 * DT_STEP) * (y_above - y_below)
            slope[2, k, x] = (0.5 * DT_STEP) * (z_above - z_below)
            penal = own * plane
            if k != 0:
                change = after * over - before * under
                add(3 - k, change if k == 1 else -change)
            if k != 1:
                y_below, y_above = along_y(penal)
                change = y_above - y_below
                add(2 - k, change if k == 2 else -change)
            if k != 2:
                z_below, z_above = along_z(penal, low, high, 3 * count_x + lane)
                change = z_above - z_below
                add(1 - k, change if k == 0 else -change)
            near = within_plane(stream[k, x + 1], low, high, 6 * count_x + lane)
            middle[k, x + 1] = (stream[k, x] + stream[k, x + 2] + near) * (1.0 / 6.0)
        for k in range(3):
            curl[k, x] = 0.5 * turned[k]


def deposited(total, k, x, count_x, half):
    window = half + ROWS
    base = (k * count_x + x) * window
    count_z = total.shape[1] // 2
    first, second = pl.ds(0, count_z), pl.ds(count_z, count_z)
    lower = total[pl.ds(base, half), first]
    shared = total[pl.ds(base + half, ROWS), first] + total[pl.ds(base, ROWS), second]
    upper = total[pl.ds(base + ROWS, half - ROWS), second]
    return jnp.concatenate([lower, shared, upper], axis=0)


def swirl(total, slope, curl, middle, x):
    _, count_x, count_y, _ = curl.shape
    moved = [deposited(total, k, x, count_x, count_y // 2) for k in range(3)]
    for k in range(3):
        stretch = moved[0] * slope[0, k, x] + moved[1] * slope[1, k, x] + moved[2] * slope[2, k, x]
        value = moved[k] + stretch + curl[k, x]
        curl[k, x] = value
        middle[k, x + 1] += value * (1.0 / 6.0)


def within_plane(plane, low, high, lane):
    y_below, y_above = along_y(plane)
    z_below, z_above = along_z(plane, low, high, lane)
    return y_below + y_above + z_below + z_above


def second_sweep(middle, vorticity, result):
    _, count_x, count_y, count_z = vorticity.shape
    at = iota((count_y, count_z), 1)
    for k in range(3):
        for x in range(count_x):
            plane = middle[k, x + 1]
            y_below, y_above = along_y(plane)
            summed = y_below + y_above
            summed = summed + jnp.where(at == 0, 0.0, pltpu.roll(plane, 1, 1))
            summed = summed + jnp.where(at == count_z - 1, 0.0, pltpu.roll(plane, count_z - 1, 1))
            if x > 0:
                summed = summed + middle[k, x]
            if x < count_x - 1:
                summed = summed + middle[k, x + 2]
            result[k, x] = (summed + vorticity[k, x]) * (1.0 / 6.0)


def pack_stream(stream, low_ref, high_ref):
    count_x = stream.shape[1] - 2
    low = high = jnp.zeros(low_ref.shape, jnp.float32)
    for k in range(3):
        for x in range(count_x):
            low = pack_column(stream[k, x + 1], k * count_x + x, False, low)
            high = pack_column(stream[k, x + 1], k * count_x + x, True, high)
    low_ref[...] = low
    high_ref[...] = high


def step(
    strength_in, fraction_in, cell_in, target_in, velocity_in, mask_in, stream_in,
    vorticity, result, x_rim, m_in,
    strength, fraction, cell, target, velocity, mask, stream,
    outgoing, arrived, total, middle, slope, z_out, z_in, m_out,
    fetch_sem, send_sem, recv_sem, face_send, face_recv, z_send, z_recv, mx_send, mx_recv, mz_send, mz_recv,
):
    groups, patches = lax.axis_size("grp"), lax.axis_size("patch")
    g, p = lax.axis_index("grp"), lax.axis_index("patch")
    shape = vorticity.shape[1:]
    count_x = shape[0]
    fetches = [
        (strength_in, strength), (fraction_in, fraction), (cell_in, cell), (target_in, target),
        (velocity_in, velocity.at[:, pl.ds(1, count_x)]),
        (mask_in, mask.at[pl.ds(1, count_x)]),
        (stream_in, stream.at[:, pl.ds(1, count_x)]),
    ]
    fetches = [pltpu.make_async_copy(a, b, fetch_sem.at[i]) for i, (a, b) in enumerate(fetches)]
    for fetch in fetches:
        fetch.start()

    barrier = pltpu.get_barrier_semaphore()

    def greet(i, carry):
        pl.semaphore_signal(barrier, inc=1, device_id={"patch": lax.rem(p + i, patches)}, device_id_type=MESH)
        return carry

    lax.fori_loop(1, patches, greet, 0)
    sides = (
        (0, "patch", p, p > 0, p - 1), (1, "patch", p, p < patches - 1, p + 1),
        (0, "grp", g, g > 0, g - 1), (1, "grp", g, g < groups - 1, g + 1),
    )
    x_sides = [(side, there, {axis: who}) for side, axis, _, there, who in sides[:2]]
    z_sides = [(side, there, {axis: who}) for side, axis, _, there, who in sides[2:]]
    for side, there, who in z_sides:
        @pl.when(there)
        def _():
            pl.semaphore_signal(barrier, inc=1, device_id=who, device_id_type=MESH)

    for side, there, who in x_sides:
        @pl.when(jnp.logical_not(there))
        def _():
            rim = side * (count_x + 1)
            empty = jnp.zeros(velocity.shape[2:], jnp.float32)
            mask[rim] = jnp.zeros(velocity.shape[2:], jnp.int32)
            for k in range(3):
                velocity[k, rim] = empty
                stream[k, rim] = empty
                x_rim[side, k] = empty
    for side, there, who in z_sides:
        @pl.when(jnp.logical_not(there))
        def _():
            z_in[side] = jnp.zeros(z_in.shape[1:], jnp.float32)
            m_in[side] = jnp.zeros(m_in.shape[1:], jnp.float32)
    total[...] = jnp.zeros_like(total)
    for fetch in fetches[:4]:
        fetch.wait()

    def remote(a, b, send, recv, who):
        return pltpu.make_async_remote_copy(
            src_ref=a, dst_ref=b, send_sem=send, recv_sem=recv, device_id=who, device_id_type=MESH
        )

    def faces(side, who):
        own, rim = 1 + side * (count_x - 1), (1 - side) * (count_x + 1)
        return [
            remote(a, b, face_send.at[side, i], face_recv.at[1 - side, i], who)
            for i, (a, b) in enumerate((
                (velocity.at[:, own], velocity.at[:, rim]),
                (mask.at[own], mask.at[rim]),
                (stream.at[:, own], stream.at[:, rim]),
            ))
        ]

    def z_face(side, who):
        return [remote(z_out.at[side], z_in.at[1 - side], z_send.at[side], z_recv.at[1 - side], who)]

    def m_face(side, who):
        own = 1 + side * (count_x - 1)
        return [remote(middle.at[:, own], x_rim.at[1 - side], mx_send.at[side], mx_recv.at[1 - side], who)]

    def mz_face(side, who):
        return [remote(m_out.at[side], m_in.at[1 - side], mz_send.at[side], mz_recv.at[1 - side], who)]

    def start(make, ways):
        for side, there, who in ways:
            @pl.when(there)
            def _():
                for copy in make(side, who):
                    copy.start()

    def finish(make, ways, sent):
        for side, there, who in ways:
            @pl.when(there)
            def _():
                for copy in make(side if sent else 1 - side, who):
                    if sent:
                        copy.wait_send()
                    else:
                        copy.wait_recv()

    def send_faces():
        for fetch in fetches[4:]:
            fetch.wait()
        pl.semaphore_wait(barrier, patches - 1 + (g > 0).astype(jnp.int32) + (g < groups - 1).astype(jnp.int32))
        start(faces, x_sides)

    route(strength, fraction, cell, target, outgoing, send_faces)

    def slots(i):
        other = lax.rem(p + i, patches)
        return remote(outgoing.at[other, pl.ds(0, 7)], arrived.at[i, pl.ds(0, 7)], send_sem.at[i], recv_sem.at[i], {"patch": other})

    def send(i, carry):
        slots(i).start()
        return carry

    lax.fori_loop(1, patches, send, 0)
    pack_faces(velocity, mask, stream, z_out)
    start(z_face, z_sides)
    deposit([outgoing[p]], total, shape)

    def take_some(first, count):
        for i in range(count):
            slots(first + i).wait_recv()
        deposit([arrived[first + i] for i in range(count)], total, shape)

    def take(i, carry):
        take_some(1 + i * GROUP, GROUP)
        return carry

    early = EARLY
    lax.fori_loop(0, early, take, 0)
    finish(faces, x_sides, False)
    finish(z_face, z_sides, False)
    prepare(velocity, mask, stream, z_in.at[0], z_in.at[1], slope, vorticity, middle)
    lax.fori_loop(early, (patches - 1) // GROUP, take, 0)

    for x in (0, count_x - 1):
        swirl(total, slope, vorticity, middle, x)
    start(m_face, x_sides)
    for x in range(1, count_x - 1):
        swirl(total, slope, vorticity, middle, x)
    pack_stream(middle, m_out.at[0], m_out.at[1])
    start(mz_face, z_sides)
    second_sweep(middle, vorticity, result)

    def sent(i, carry):
        slots(i).wait_send()
        return carry

    lax.fori_loop(1, patches, sent, 0)
    finish(faces, x_sides, True)
    finish(z_face, z_sides, True)
    finish(m_face, x_sides, True)
    finish(mz_face, z_sides, True)
    finish(m_face, x_sides, False)
    finish(mz_face, z_sides, False)


GROUP = 3
EARLY = 2


def write_out(vorticity, inner, x_rim, m_in, vorticity_out, result_out, result, sem):
    _, count_x, count_y, count_z = inner.shape
    written = pltpu.make_async_copy(vorticity, vorticity_out, sem.at[0])
    written.start()
    at = iota((count_y, count_z), 1)
    low, high = m_in[0], m_in[1]
    for k in range(3):
        for x in range(count_x):
            lane = k * count_x + x
            from_low = pltpu.roll(low, (count_z - lane) % count_z, 1) if lane else low
            from_high = pltpu.roll(high, count_z - 1 - lane, 1)
            extra = jnp.where(at == 0, from_low, 0.0) + jnp.where(at == count_z - 1, from_high, 0.0)
            if x == 0:
                extra = extra + x_rim[0, k]
            if x == count_x - 1:
                extra = extra + x_rim[1, k]
            result[k, x] = inner[k, x] + extra * (1.0 / 6.0)
    solved = pltpu.make_async_copy(result, result_out, sem.at[1])
    solved.start()
    written.wait()
    solved.wait()


def shards(strength, fraction, cell, patch_of, velocity, body_mask, stream_prev):
    rows = patch_of.shape[0]
    patches = lax.axis_size("patch")
    capacity = 2 * rows // patches
    parts, count_x, count_y, count_z = velocity.shape
    plane = (count_y, count_z)
    room = lambda *shape: pltpu.VMEM(shape, jnp.float32)
    ints = lambda *shape: pltpu.VMEM(shape, jnp.int32)
    dma = lambda *shape: pltpu.SemaphoreType.DMA(shape)
    whole = velocity.shape
    taken = (strength, fraction, cell.reshape(1, rows), patch_of.reshape(1, rows), velocity, body_mask, stream_prev)
    made = pl.pallas_call(
        step,
        out_shape=[room(*whole), room(*whole), room(2, parts, *plane), room(2, *plane)],
        in_specs=[HBM] * 7,
        out_specs=[VMEM] * 4,
        scratch_shapes=[
            room(3, rows), room(3, rows), ints(1, rows), ints(1, rows),
            room(parts, count_x + 2, *plane), ints(count_x + 2, *plane), room(parts, count_x + 2, *plane),
            room(patches, ROWS, capacity), room(patches, ROWS, capacity),
            room(parts * count_x * (count_y // 2 + ROWS), 2 * count_z), room(parts, count_x + 2, *plane),
            room(3, *whole),
            room(2, *plane), room(2, *plane), room(2, *plane),
            dma(7), dma(patches), dma(patches), dma(2, 3), dma(2, 3),
            dma(2), dma(2), dma(2), dma(2), dma(2), dma(2),
        ],
        compiler_params=pltpu.CompilerParams(
            collective_id=0, has_side_effects=True, vmem_limit_bytes=50 * 2**20
        ),
    )(*[pltpu.with_memory_space_constraint(array, pltpu.HBM) for array in taken])
    return tuple(pl.pallas_call(
        write_out,
        out_shape=[jax.ShapeDtypeStruct(whole, jnp.float32)] * 2,
        in_specs=[VMEM] * 4,
        out_specs=[HBM] * 2,
        scratch_shapes=[room(*whole), dma(2)],
    )(*[pltpu.with_memory_space_constraint(array, pltpu.VMEM) for array in made]))


def solution(mesh):
    in_specs = (
        P(None, ("grp", "patch")),
        P(None, ("grp", "patch")),
        P(("grp", "patch")),
        P(("grp", "patch"), None),
        P(None, "patch", None, "grp"),
        P("patch", None, "grp"),
        P(None, "patch", None, "grp"),
    )
    out_specs = (P(None, "patch", None, "grp"), P(None, "patch", None, "grp"))
    return jax.shard_map(shards, mesh=mesh, in_specs=in_specs, out_specs=out_specs, check_vma=False)
```

```python
import jax
import jax.numpy as jnp
from jax import lax
from jax.experimental import pallas as pl
from jax.experimental.pallas import tpu as pltpu
from jax.sharding import PartitionSpec as P

DT_STEP = 0.5
PEN_GAIN = 0.8
ROWS = 8
HBM = pl.BlockSpec(memory_space=pltpu.HBM)
VMEM = pl.BlockSpec(memory_space=pltpu.VMEM)
MESH = pl.DeviceIdType.MESH
NT = (((1,), (1,)), ((), ()))


def kernel(distance):
    d = jnp.minimum(jnp.abs(distance), 2.0)
    near_part = 1.0 + d * d * (1.5 * d - 2.5)
    t = 2.0 - d
    return jnp.where(d < 1.0, near_part, 0.5 * t * t * (1.0 - d))


def iota(shape, dim):
    return lax.broadcasted_iota(jnp.int32, shape, dim)


def pack_column(plane, lane, high, packed):
    width = plane.shape[1]
    turn = (lane + 1) % width if high else lane
    moved = pltpu.roll(plane, turn, 1) if turn else plane
    return jnp.where(iota(plane.shape, 1) == lane, moved, packed)


def along_z(plane, low, high, lane):
    width = plane.shape[1]
    at = iota(plane.shape, 1)
    from_low = pltpu.roll(low, (width - lane) % width, 1) if lane else low
    turn = width - 1 - lane
    from_high = pltpu.roll(high, turn, 1) if turn else high
    below = jnp.where(at == 0, from_low, pltpu.roll(plane, 1, 1))
    above = jnp.where(at == width - 1, from_high, pltpu.roll(plane, width - 1, 1))
    return below, above


def along_y(plane):
    height = plane.shape[0]
    at = iota(plane.shape, 0)
    below = jnp.where(at == 0, 0.0, pltpu.roll(plane, 1, 0))
    above = jnp.where(at == height - 1, 0.0, pltpu.roll(plane, height - 1, 0))
    return below, above


def rank(target, patches, chunk):
    turns = target.shape[1] // chunk
    tri = (iota((chunk, chunk), 0) < iota((chunk, chunk), 1)).astype(jnp.float32).astype(jnp.bfloat16)
    chosen = [
        (iota((patches, chunk), 0) == target[:, pl.ds(turn * chunk, chunk)]).astype(jnp.float32) for turn in range(turns)
    ]
    stacked = jnp.concatenate(chosen, axis=0).astype(jnp.bfloat16)
    prefix = jnp.dot(stacked, tri, preferred_element_type=jnp.float32)
    running = jnp.zeros((patches, 1), jnp.float32)
    result = []
    for turn in range(turns):
        named = chosen[turn]
        before = prefix[turn * patches : (turn + 1) * patches] + running
        running = running + jnp.sum(named, axis=1, keepdims=True)
        result.append(jnp.sum(before * named, axis=0, keepdims=True).astype(jnp.int32))
    return result


def route(strength, fraction, cell, target, out, amid):
    rows = strength.shape[1]
    patches, _, capacity = out.shape
    chunk = min(512, rows)
    turns = rows // chunk
    places = rank(target, patches, chunk)
    for turn in range(turns):
        if turn == turns // 2:
            amid()
        at = pl.ds(turn * chunk, chunk)
        named = target[:, at]
        slots = (iota((capacity, chunk), 0) == places[turn]).astype(jnp.float32).astype(jnp.bfloat16)
        value = jnp.concatenate(
            [strength[:, at], fraction[:, at], cell[:, at].astype(jnp.float32), jnp.zeros((1, chunk), jnp.float32)],
            axis=0,
        )
        coarse = value.astype(jnp.bfloat16).astype(jnp.float32)
        fine = value - coarse
        pieces = []
        for p in range(patches):
            hit = named == p
            pieces.extend((jnp.where(hit, coarse, 0.0), jnp.where(hit, fine, 0.0)))
        left = jnp.concatenate(pieces, axis=0).astype(jnp.bfloat16)
        product = lax.dot_general(left, slots, NT, preferred_element_type=jnp.float32)
        product = product.reshape(patches, 2 * ROWS, capacity)
        moved = product[:, :ROWS] + product[:, ROWS:]
        if turn == 0:
            out[...] = moved
        else:
            out[...] += moved


def pack_faces(velocity, mask, stream, out):
    count_x = velocity.shape[1] - 2
    low = high = jnp.zeros(out.shape[1:], jnp.float32)
    for k in range(3):
        for x in range(count_x):
            speed = velocity[k, x + 1]
            penal = -PEN_GAIN * mask[x + 1].astype(jnp.float32) * speed
            for part, plane in enumerate((speed, penal, stream[k, x + 1])):
                lane = (part * 3 + k) * count_x + x
                low = pack_column(plane, lane, False, low)
                high = pack_column(plane, lane, True, high)
    out[0] = low
    out[1] = high


def spread(pattern, group, count):
    low, high = pattern[:ROWS], pattern[ROWS:]
    hits = [group == at for at in range(count)]
    result = []
    for at in range(count):
        piece = jnp.where(hits[at], low, 0.0)
        result.append(jnp.where(hits[at - 1], high, piece) if at else piece)
    return result


def deposit_operands(data, shape):
    count_x, count_y, count_z = shape
    span_y, span_z = count_y - 3, count_z - 3
    half = count_y // 2
    slots = data.shape[1]
    cell = data[6:7]
    quot_x = ((cell + 0.5) * (1.0 / (span_y * span_z))).astype(jnp.int32).astype(jnp.float32)
    rest = cell - quot_x * (span_y * span_z)
    quot_y = ((rest + 0.5) * (1.0 / span_z)).astype(jnp.int32)
    quot_z = (rest - quot_y.astype(jnp.float32) * span_z).astype(jnp.int32)
    upper = quot_y >= half
    quot_y = jnp.where(upper, quot_y - half, quot_y)

    def pattern(quot, part):
        group = lax.shift_right_logical(quot, 3)
        first = (quot - group * ROWS).astype(jnp.float32) + 1.0
        away = iota((2 * ROWS, slots), 0).astype(jnp.float32) - first
        return group, kernel(away - part)

    weight_x = kernel((iota((count_x, slots), 0).astype(jnp.float32) - (quot_x + 1.0)) - data[3:4])
    group_y, weight_y = pattern(quot_y, data[4:5])
    group_z, weight_z = pattern(quot_z, data[5:6])
    window = spread(weight_y, group_y, half // ROWS + 1)
    depth = jnp.concatenate(spread(weight_z, group_z, count_z // ROWS), axis=0)
    depth = jnp.concatenate([jnp.where(upper, 0.0, depth), jnp.where(upper, depth, 0.0)], axis=0).astype(jnp.bfloat16)
    pieces = []
    for k in range(3):
        scaled = data[k : k + 1] * weight_x
        for x in range(count_x):
            line = scaled[x : x + 1]
            pieces.extend(line * piece for piece in window)
    return jnp.concatenate(pieces, axis=0).astype(jnp.bfloat16), depth


def deposit(blocks, total, shape):
    pairs = [deposit_operands(block, shape) for block in blocks]
    left = jnp.concatenate([pair[0] for pair in pairs], axis=1)
    right = jnp.concatenate([pair[1] for pair in pairs], axis=1)
    total[...] += lax.dot_general(left, right, NT, preferred_element_type=jnp.float32)


def prepare(velocity, mask, stream, z_low, z_high, slope, curl, middle, planes):
    _, count_x, count_y, _ = curl.shape
    low, high = z_low[...], z_high[...]
    for x in planes:
        before, own, after = [-PEN_GAIN * mask[x + i].astype(jnp.float32) for i in range(3)]
        turned = [None] * 3

        def add(k, change):
            turned[k] = change if turned[k] is None else turned[k] + change

        for k in range(3):
            under, plane, over = [velocity[k, x + i] for i in range(3)]
            y_below, y_above = along_y(plane)
            lane = k * count_x + x
            z_below, z_above = along_z(plane, low, high, lane)
            slope[0, k, x] = (0.5 * DT_STEP) * (over - under)
            slope[1, k, x] = (0.5 * DT_STEP) * (y_above - y_below)
            slope[2, k, x] = (0.5 * DT_STEP) * (z_above - z_below)
            penal = own * plane
            if k != 0:
                change = after * over - before * under
                add(3 - k, change if k == 1 else -change)
            if k != 1:
                y_below, y_above = along_y(penal)
                change = y_above - y_below
                add(2 - k, change if k == 2 else -change)
            if k != 2:
                z_below, z_above = along_z(penal, low, high, 3 * count_x + lane)
                change = z_above - z_below
                add(1 - k, change if k == 0 else -change)
            near = within_plane(stream[k, x + 1], low, high, 6 * count_x + lane)
            middle[k, x + 1] = (stream[k, x] + stream[k, x + 2] + near) * (1.0 / 6.0)
        for k in range(3):
            curl[k, x] = 0.5 * turned[k]


def deposited(total, k, x, count_x, half):
    window = half + ROWS
    base = (k * count_x + x) * window
    count_z = total.shape[1] // 2
    first, second = pl.ds(0, count_z), pl.ds(count_z, count_z)
    lower = total[pl.ds(base, half), first]
    shared = total[pl.ds(base + half, ROWS), first] + total[pl.ds(base, ROWS), second]
    upper = total[pl.ds(base + ROWS, half - ROWS), second]
    return jnp.concatenate([lower, shared, upper], axis=0)


def swirl(total, slope, curl, middle, x):
    _, count_x, count_y, _ = curl.shape
    moved = [deposited(total, k, x, count_x, count_y // 2) for k in range(3)]
    for k in range(3):
        stretch = moved[0] * slope[0, k, x] + moved[1] * slope[1, k, x] + moved[2] * slope[2, k, x]
        value = moved[k] + stretch + curl[k, x]
        curl[k, x] = value
        middle[k, x + 1] += value * (1.0 / 6.0)


def within_plane(plane, low, high, lane):
    y_below, y_above = along_y(plane)
    z_below, z_above = along_z(plane, low, high, lane)
    return y_below + y_above + z_below + z_above


def second_sweep(middle, vorticity, result):
    _, count_x, count_y, count_z = vorticity.shape
    at = iota((count_y, count_z), 1)
    for k in range(3):
        for x in range(count_x):
            plane = middle[k, x + 1]
            y_below, y_above = along_y(plane)
            summed = y_below + y_above
            summed = summed + jnp.where(at == 0, 0.0, pltpu.roll(plane, 1, 1))
            summed = summed + jnp.where(at == count_z - 1, 0.0, pltpu.roll(plane, count_z - 1, 1))
            if x > 0:
                summed = summed + middle[k, x]
            if x < count_x - 1:
                summed = summed + middle[k, x + 2]
            result[k, x] = (summed + vorticity[k, x]) * (1.0 / 6.0)


def pack_stream(stream, low_ref, high_ref):
    count_x = stream.shape[1] - 2
    low = high = jnp.zeros(low_ref.shape, jnp.float32)
    for k in range(3):
        for x in range(count_x):
            low = pack_column(stream[k, x + 1], k * count_x + x, False, low)
            high = pack_column(stream[k, x + 1], k * count_x + x, True, high)
    low_ref[...] = low
    high_ref[...] = high


def step(
    strength_in, fraction_in, cell_in, target_in, velocity_in, mask_in, stream_in,
    vorticity, result, x_rim, m_in,
    strength, fraction, cell, target, velocity, mask, stream,
    outgoing, arrived, total, middle, slope, z_out, z_in, m_out,
    fetch_sem, send_sem, recv_sem, face_send, face_recv, z_send, z_recv, mx_send, mx_recv, mz_send, mz_recv,
):
    groups, patches = lax.axis_size("grp"), lax.axis_size("patch")
    g, p = lax.axis_index("grp"), lax.axis_index("patch")
    shape = vorticity.shape[1:]
    count_x = shape[0]
    fetches = [
        (strength_in, strength), (fraction_in, fraction), (cell_in, cell), (target_in, target),
        (velocity_in, velocity.at[:, pl.ds(1, count_x)]),
        (mask_in, mask.at[pl.ds(1, count_x)]),
        (stream_in, stream.at[:, pl.ds(1, count_x)]),
    ]
    fetches = [pltpu.make_async_copy(a, b, fetch_sem.at[i]) for i, (a, b) in enumerate(fetches)]
    for fetch in fetches:
        fetch.start()

    barrier = pltpu.get_barrier_semaphore()

    def greet(i, carry):
        pl.semaphore_signal(barrier, inc=1, device_id={"patch": lax.rem(p + i, patches)}, device_id_type=MESH)
        return carry

    lax.fori_loop(1, patches, greet, 0)
    sides = (
        (0, "patch", p, p > 0, p - 1), (1, "patch", p, p < patches - 1, p + 1),
        (0, "grp", g, g > 0, g - 1), (1, "grp", g, g < groups - 1, g + 1),
    )
    x_sides = [(side, there, {axis: who}) for side, axis, _, there, who in sides[:2]]
    z_sides = [(side, there, {axis: who}) for side, axis, _, there, who in sides[2:]]
    for side, there, who in z_sides:
        @pl.when(there)
        def _():
            pl.semaphore_signal(barrier, inc=1, device_id=who, device_id_type=MESH)

    for side, there, who in x_sides:
        @pl.when(jnp.logical_not(there))
        def _():
            rim = side * (count_x + 1)
            empty = jnp.zeros(velocity.shape[2:], jnp.float32)
            mask[rim] = jnp.zeros(velocity.shape[2:], jnp.int32)
            for k in range(3):
                velocity[k, rim] = empty
                stream[k, rim] = empty
                x_rim[side, k] = empty
    for side, there, who in z_sides:
        @pl.when(jnp.logical_not(there))
        def _():
            z_in[side] = jnp.zeros(z_in.shape[1:], jnp.float32)
            m_in[side] = jnp.zeros(m_in.shape[1:], jnp.float32)
    total[...] = jnp.zeros_like(total)
    for fetch in fetches[:4]:
        fetch.wait()

    def remote(a, b, send, recv, who):
        return pltpu.make_async_remote_copy(
            src_ref=a, dst_ref=b, send_sem=send, recv_sem=recv, device_id=who, device_id_type=MESH
        )

    def faces(side, who):
        own, rim = 1 + side * (count_x - 1), (1 - side) * (count_x + 1)
        return [
            remote(a, b, face_send.at[side, i], face_recv.at[1 - side, i], who)
            for i, (a, b) in enumerate((
                (velocity.at[:, own], velocity.at[:, rim]),
                (mask.at[own], mask.at[rim]),
                (stream.at[:, own], stream.at[:, rim]),
            ))
        ]

    def z_face(side, who):
        return [remote(z_out.at[side], z_in.at[1 - side], z_send.at[side], z_recv.at[1 - side], who)]

    def m_face(side, who):
        own = 1 + side * (count_x - 1)
        return [remote(middle.at[:, own], x_rim.at[1 - side], mx_send.at[side], mx_recv.at[1 - side], who)]

    def mz_face(side, who):
        return [remote(m_out.at[side], m_in.at[1 - side], mz_send.at[side], mz_recv.at[1 - side], who)]

    def start(make, ways):
        for side, there, who in ways:
            @pl.when(there)
            def _():
                for copy in make(side, who):
                    copy.start()

    def finish(make, ways, sent):
        for side, there, who in ways:
            @pl.when(there)
            def _():
                for copy in make(side if sent else 1 - side, who):
                    if sent:
                        copy.wait_send()
                    else:
                        copy.wait_recv()

    def send_faces():
        for fetch in fetches[4:]:
            fetch.wait()
        pl.semaphore_wait(barrier, patches - 1 + (g > 0).astype(jnp.int32) + (g < groups - 1).astype(jnp.int32))

    route(strength, fraction, cell, target, outgoing, lambda: None)
    send_faces()

    def peer(i):
        return i + (i >= p).astype(jnp.int32)

    def going(i):
        other = peer(i)
        return remote(outgoing.at[other, pl.ds(0, 7)], arrived.at[p, pl.ds(0, 7)], send_sem.at[i], recv_sem.at[p], {"patch": other})

    def coming(i):
        other = peer(i)
        return remote(outgoing.at[other, pl.ds(0, 7)], arrived.at[other, pl.ds(0, 7)], send_sem.at[i], recv_sem.at[other], {"patch": other})

    def send(i, carry):
        going(i).start()
        return carry

    lax.fori_loop(0, patches - 1, send, 0)
    start(faces, x_sides)
    pack_faces(velocity, mask, stream, z_out)
    start(z_face, z_sides)
    deposit([outgoing[p]], total, shape)

    def take_some(first, count):
        for i in range(count):
            coming(first + i).wait_recv()
        deposit([arrived[peer(first + i)] for i in range(count)], total, shape)

    def take(i, carry):
        take_some(i * GROUP, GROUP)
        return carry

    early = EARLY
    lax.fori_loop(0, early, take, 0)
    finish(z_face, z_sides, False)
    prepare(velocity, mask, stream, z_in.at[0], z_in.at[1], slope, vorticity, middle, range(1, count_x - 1))
    lax.fori_loop(early, (patches - 1) // GROUP, take, 0)
    finish(faces, x_sides, False)
    prepare(velocity, mask, stream, z_in.at[0], z_in.at[1], slope, vorticity, middle, (0, count_x - 1))
    for x in (0, count_x - 1):
        swirl(total, slope, vorticity, middle, x)
    start(m_face, x_sides)
    for x in range(1, count_x - 1):
        swirl(total, slope, vorticity, middle, x)
    pack_stream(middle, m_out.at[0], m_out.at[1])
    start(mz_face, z_sides)
    second_sweep(middle, vorticity, result)

    def sent(i, carry):
        going(i).wait_send()
        return carry

    lax.fori_loop(0, patches - 1, sent, 0)
    finish(faces, x_sides, True)
    finish(z_face, z_sides, True)
    finish(m_face, x_sides, True)
    finish(mz_face, z_sides, True)
    finish(m_face, x_sides, False)
    finish(mz_face, z_sides, False)


GROUP = 3
EARLY = 3


def write_out(vorticity, inner, x_rim, m_in, vorticity_out, result_out, result, sem):
    _, count_x, count_y, count_z = inner.shape
    written = pltpu.make_async_copy(vorticity, vorticity_out, sem.at[0])
    written.start()
    at = iota((count_y, count_z), 1)
    low, high = m_in[0], m_in[1]
    for k in range(3):
        for x in range(count_x):
            lane = k * count_x + x
            from_low = pltpu.roll(low, (count_z - lane) % count_z, 1) if lane else low
            from_high = pltpu.roll(high, count_z - 1 - lane, 1)
            extra = jnp.where(at == 0, from_low, 0.0) + jnp.where(at == count_z - 1, from_high, 0.0)
            if x == 0:
                extra = extra + x_rim[0, k]
            if x == count_x - 1:
                extra = extra + x_rim[1, k]
            result[k, x] = inner[k, x] + extra * (1.0 / 6.0)
    solved = pltpu.make_async_copy(result, result_out, sem.at[1])
    solved.start()
    written.wait()
    solved.wait()


def shards(strength, fraction, cell, patch_of, velocity, body_mask, stream_prev):
    rows = patch_of.shape[0]
    patches = lax.axis_size("patch")
    capacity = 2 * rows // patches
    parts, count_x, count_y, count_z = velocity.shape
    plane = (count_y, count_z)
    room = lambda *shape: pltpu.VMEM(shape, jnp.float32)
    ints = lambda *shape: pltpu.VMEM(shape, jnp.int32)
    dma = lambda *shape: pltpu.SemaphoreType.DMA(shape)
    whole = velocity.shape
    taken = (strength, fraction, cell.reshape(1, rows), patch_of.reshape(1, rows), velocity, body_mask, stream_prev)
    made = pl.pallas_call(
        step,
        out_shape=[room(*whole), room(*whole), room(2, parts, *plane), room(2, *plane)],
        in_specs=[HBM] * 7,
        out_specs=[VMEM] * 4,
        scratch_shapes=[
            room(3, rows), room(3, rows), ints(1, rows), ints(1, rows),
            room(parts, count_x + 2, *plane), ints(count_x + 2, *plane), room(parts, count_x + 2, *plane),
            room(patches, ROWS, capacity), room(patches, ROWS, capacity),
            room(parts * count_x * (count_y // 2 + ROWS), 2 * count_z), room(parts, count_x + 2, *plane),
            room(3, *whole),
            room(2, *plane), room(2, *plane), room(2, *plane),
            dma(7), dma(patches), dma(patches), dma(2, 3), dma(2, 3),
            dma(2), dma(2), dma(2), dma(2), dma(2), dma(2),
        ],
        compiler_params=pltpu.CompilerParams(
            collective_id=0, has_side_effects=True, vmem_limit_bytes=50 * 2**20
        ),
    )(*[pltpu.with_memory_space_constraint(array, pltpu.HBM) for array in taken])
    return tuple(pl.pallas_call(
        write_out,
        out_shape=[jax.ShapeDtypeStruct(whole, jnp.float32)] * 2,
        in_specs=[VMEM] * 4,
        out_specs=[HBM] * 2,
        scratch_shapes=[room(*whole), dma(2)],
    )(*[pltpu.with_memory_space_constraint(array, pltpu.VMEM) for array in made]))


def solution(mesh):
    in_specs = (
        P(None, ("grp", "patch")),
        P(None, ("grp", "patch")),
        P(("grp", "patch")),
        P(("grp", "patch"), None),
        P(None, "patch", None, "grp"),
        P("patch", None, "grp"),
        P(None, "patch", None, "grp"),
    )
    out_specs = (P(None, "patch", None, "grp"), P(None, "patch", None, "grp"))
    return jax.shard_map(shards, mesh=mesh, in_specs=in_specs, out_specs=out_specs, check_vma=False)
```

```python
import jax
import jax.numpy as jnp
from jax import lax
from jax.experimental import pallas as pl
from jax.experimental.pallas import tpu as pltpu
from jax.sharding import PartitionSpec as P

DT_STEP = 0.5
PEN_GAIN = 0.8
ROWS = 8
HBM = pl.BlockSpec(memory_space=pltpu.HBM)
VMEM = pl.BlockSpec(memory_space=pltpu.VMEM)
MESH = pl.DeviceIdType.MESH
NT = (((1,), (1,)), ((), ()))


def kernel(distance):
    d = jnp.minimum(jnp.abs(distance), 2.0)
    near_part = 1.0 + d * d * (1.5 * d - 2.5)
    t = 2.0 - d
    return jnp.where(d < 1.0, near_part, 0.5 * t * t * (1.0 - d))


def iota(shape, dim):
    return lax.broadcasted_iota(jnp.int32, shape, dim)


def pack_edges(planes):
    width = planes[0].shape[1]
    pair = lax.shift_right_logical(iota(planes[0].shape, 1), 1)
    packed = jnp.zeros(planes[0].shape, jnp.float32)
    for i, plane in enumerate(planes):
        packed = jnp.where(pair == i, pltpu.roll(plane, (2 * i + 1) % width, 1), packed)
    return packed


def join_edges(from_low, from_high):
    width = from_low.shape[1]
    return jnp.where(iota(from_low.shape, 1) % 2 == 0, from_low, pltpu.roll(from_high, width - 2, 1))


def edge_of(joined, i):
    width = joined.shape[1]
    return pltpu.roll(joined, width - 2 * i, 1) if i else joined


def along_z(plane, edge):
    width = plane.shape[1]
    at = iota(plane.shape, 1)
    below = jnp.where(at == 0, edge, pltpu.roll(plane, 1, 1))
    above = jnp.where(at == width - 1, edge, pltpu.roll(plane, width - 1, 1))
    return below, above


def along_y(plane):
    height = plane.shape[0]
    at = iota(plane.shape, 0)
    below = jnp.where(at == 0, 0.0, pltpu.roll(plane, 1, 0))
    above = jnp.where(at == height - 1, 0.0, pltpu.roll(plane, height - 1, 0))
    return below, above


def rank(target, patches, chunk):
    turns = target.shape[1] // chunk
    tri = (iota((chunk, chunk), 0) < iota((chunk, chunk), 1)).astype(jnp.float32).astype(jnp.bfloat16)
    chosen = [
        (iota((patches, chunk), 0) == target[:, pl.ds(turn * chunk, chunk)]).astype(jnp.float32) for turn in range(turns)
    ]
    stacked = jnp.concatenate(chosen, axis=0).astype(jnp.bfloat16)
    prefix = jnp.dot(stacked, tri, preferred_element_type=jnp.float32)
    running = jnp.zeros((patches, 1), jnp.float32)
    result = []
    for turn in range(turns):
        named = chosen[turn]
        before = prefix[turn * patches : (turn + 1) * patches] + running
        running = running + jnp.sum(named, axis=1, keepdims=True)
        result.append(jnp.sum(before * named, axis=0, keepdims=True).astype(jnp.int32))
    return result


def route(strength, fraction, cell, target, out, amid):
    rows = strength.shape[1]
    patches, _, capacity = out.shape
    chunk = min(512, rows)
    turns = rows // chunk
    places = rank(target, patches, chunk)
    for turn in range(turns):
        if turn == turns // 2:
            amid()
        at = pl.ds(turn * chunk, chunk)
        named = target[:, at]
        slots = (iota((capacity, chunk), 0) == places[turn]).astype(jnp.float32).astype(jnp.bfloat16)
        value = jnp.concatenate(
            [strength[:, at], fraction[:, at], cell[:, at].astype(jnp.float32), jnp.zeros((1, chunk), jnp.float32)],
            axis=0,
        )
        coarse = value.astype(jnp.bfloat16).astype(jnp.float32)
        fine = value - coarse
        pieces = []
        for p in range(patches):
            hit = named == p
            pieces.extend((jnp.where(hit, coarse, 0.0), jnp.where(hit, fine, 0.0)))
        left = jnp.concatenate(pieces, axis=0).astype(jnp.bfloat16)
        product = lax.dot_general(left, slots, NT, preferred_element_type=jnp.float32)
        product = product.reshape(patches, 2 * ROWS, capacity)
        moved = product[:, :ROWS] + product[:, ROWS:]
        if turn == 0:
            out[...] = moved
        else:
            out[...] += moved


def pack_faces(velocity, mask, stream, out):
    count_x = velocity.shape[1] - 2
    inner = range(1, count_x + 1)
    planes = [velocity[k, x] for k in range(3) for x in inner]
    planes.extend(-PEN_GAIN * mask[x].astype(jnp.float32) for x in inner)
    planes.extend(stream[k, x] for k in range(3) for x in inner)
    out[...] = pack_edges(planes)


def spread(pattern, group, count):
    low, high = pattern[:ROWS], pattern[ROWS:]
    hits = [group == at for at in range(count)]
    result = []
    for at in range(count):
        piece = jnp.where(hits[at], low, 0.0)
        result.append(jnp.where(hits[at - 1], high, piece) if at else piece)
    return result


def deposit_operands(data, shape):
    count_x, count_y, count_z = shape
    span_y, span_z = count_y - 3, count_z - 3
    half = count_y // 2
    slots = data.shape[1]
    cell = data[6:7]
    quot_x = ((cell + 0.5) * (1.0 / (span_y * span_z))).astype(jnp.int32).astype(jnp.float32)
    rest = cell - quot_x * (span_y * span_z)
    quot_y = ((rest + 0.5) * (1.0 / span_z)).astype(jnp.int32)
    quot_z = (rest - quot_y.astype(jnp.float32) * span_z).astype(jnp.int32)
    upper = quot_y >= half
    quot_y = jnp.where(upper, quot_y - half, quot_y)

    def pattern(quot, part):
        group = lax.shift_right_logical(quot, 3)
        first = (quot - group * ROWS).astype(jnp.float32) + 1.0
        away = iota((2 * ROWS, slots), 0).astype(jnp.float32) - first
        return group, kernel(away - part)

    weight_x = kernel((iota((count_x, slots), 0).astype(jnp.float32) - (quot_x + 1.0)) - data[3:4])
    group_y, weight_y = pattern(quot_y, data[4:5])
    group_z, weight_z = pattern(quot_z, data[5:6])
    window = spread(weight_y, group_y, half // ROWS + 1)
    depth = jnp.concatenate(spread(weight_z, group_z, count_z // ROWS), axis=0)
    depth = jnp.concatenate([jnp.where(upper, 0.0, depth), jnp.where(upper, depth, 0.0)], axis=0).astype(jnp.bfloat16)
    pieces = []
    for k in range(3):
        scaled = data[k : k + 1] * weight_x
        for x in range(count_x):
            line = scaled[x : x + 1]
            pieces.extend(line * piece for piece in window)
    return jnp.concatenate(pieces, axis=0).astype(jnp.bfloat16), depth


def deposit(blocks, total, shape):
    pairs = [deposit_operands(block, shape) for block in blocks]
    left = jnp.concatenate([pair[0] for pair in pairs], axis=1)
    right = jnp.concatenate([pair[1] for pair in pairs], axis=1)
    total[...] += lax.dot_general(left, right, NT, preferred_element_type=jnp.float32)


def prepare(velocity, mask, stream, z_in, slope, curl, middle, planes):
    _, count_x, count_y, _ = curl.shape
    joined = join_edges(z_in[0], z_in[1])
    for x in planes:
        own_edge = edge_of(joined, 3 * count_x + x)
        before, own, after = [-PEN_GAIN * mask[x + i].astype(jnp.float32) for i in range(3)]
        turned = [None] * 3

        def add(k, change):
            turned[k] = change if turned[k] is None else turned[k] + change

        for k in range(3):
            under, plane, over = [velocity[k, x + i] for i in range(3)]
            y_below, y_above = along_y(plane)
            lane = k * count_x + x
            edge = edge_of(joined, lane)
            z_below, z_above = along_z(plane, edge)
            slope[0, k, x] = (0.5 * DT_STEP) * (over - under)
            slope[1, k, x] = (0.5 * DT_STEP) * (y_above - y_below)
            slope[2, k, x] = (0.5 * DT_STEP) * (z_above - z_below)
            penal = own * plane
            if k != 0:
                change = after * over - before * under
                add(3 - k, change if k == 1 else -change)
            if k != 1:
                y_below, y_above = along_y(penal)
                change = y_above - y_below
                add(2 - k, change if k == 2 else -change)
            if k != 2:
                z_below, z_above = along_z(penal, own_edge * edge)
                change = z_above - z_below
                add(1 - k, change if k == 0 else -change)
            near = within_plane(stream[k, x + 1], edge_of(joined, 4 * count_x + lane))
            middle[k, x + 1] = (stream[k, x] + stream[k, x + 2] + near) * (1.0 / 6.0)
        for k in range(3):
            curl[k, x] = 0.5 * turned[k]


def deposited(total, k, x, count_x, half):
    window = half + ROWS
    base = (k * count_x + x) * window
    count_z = total.shape[1] // 2
    first, second = pl.ds(0, count_z), pl.ds(count_z, count_z)
    lower = total[pl.ds(base, half), first]
    shared = total[pl.ds(base + half, ROWS), first] + total[pl.ds(base, ROWS), second]
    upper = total[pl.ds(base + ROWS, half - ROWS), second]
    return jnp.concatenate([lower, shared, upper], axis=0)


def swirl(total, slope, curl, middle, x):
    _, count_x, count_y, _ = curl.shape
    moved = [deposited(total, k, x, count_x, count_y // 2) for k in range(3)]
    for k in range(3):
        stretch = moved[0] * slope[0, k, x] + moved[1] * slope[1, k, x] + moved[2] * slope[2, k, x]
        value = moved[k] + stretch + curl[k, x]
        curl[k, x] = value
        middle[k, x + 1] += value * (1.0 / 6.0)


def within_plane(plane, edge):
    y_below, y_above = along_y(plane)
    z_below, z_above = along_z(plane, edge)
    return y_below + y_above + z_below + z_above


def second_sweep(middle, vorticity, result):
    _, count_x, count_y, count_z = vorticity.shape
    empty = jnp.zeros((count_y, count_z), jnp.float32)
    for k in range(3):
        for x in range(count_x):
            summed = within_plane(middle[k, x + 1], empty)
            if x > 0:
                summed = summed + middle[k, x]
            if x < count_x - 1:
                summed = summed + middle[k, x + 2]
            result[k, x] = (summed + vorticity[k, x]) * (1.0 / 6.0)


def pack_stream(stream, out):
    count_x = stream.shape[1] - 2
    out[...] = pack_edges([stream[k, x] for k in range(3) for x in range(1, count_x + 1)])


def step(
    strength_in, fraction_in, cell_in, target_in, velocity_in, mask_in, stream_in,
    vorticity, result, x_rim, m_in,
    strength, fraction, cell, target, velocity, mask, stream,
    outgoing, arrived, total, middle, slope, z_out, z_in, m_out,
    fetch_sem, send_sem, recv_sem, face_send, face_recv, z_send, z_recv, mx_send, mx_recv, mz_send, mz_recv,
):
    groups, patches = lax.axis_size("grp"), lax.axis_size("patch")
    g, p = lax.axis_index("grp"), lax.axis_index("patch")
    shape = vorticity.shape[1:]
    count_x = shape[0]
    fetches = [
        (strength_in, strength), (fraction_in, fraction), (cell_in, cell), (target_in, target),
        (velocity_in, velocity.at[:, pl.ds(1, count_x)]),
        (mask_in, mask.at[pl.ds(1, count_x)]),
        (stream_in, stream.at[:, pl.ds(1, count_x)]),
    ]
    fetches = [pltpu.make_async_copy(a, b, fetch_sem.at[i]) for i, (a, b) in enumerate(fetches)]
    for fetch in fetches:
        fetch.start()

    barrier = pltpu.get_barrier_semaphore()

    def greet(i, carry):
        pl.semaphore_signal(barrier, inc=1, device_id={"patch": lax.rem(p + i, patches)}, device_id_type=MESH)
        return carry

    lax.fori_loop(1, patches, greet, 0)
    sides = (
        (0, "patch", p, p > 0, p - 1), (1, "patch", p, p < patches - 1, p + 1),
        (0, "grp", g, g > 0, g - 1), (1, "grp", g, g < groups - 1, g + 1),
    )
    x_sides = [(side, there, {axis: who}) for side, axis, _, there, who in sides[:2]]
    z_sides = [(side, there, {axis: who}) for side, axis, _, there, who in sides[2:]]
    for side, there, who in z_sides:
        @pl.when(there)
        def _():
            pl.semaphore_signal(barrier, inc=1, device_id=who, device_id_type=MESH)

    for side, there, who in x_sides:
        @pl.when(jnp.logical_not(there))
        def _():
            rim = side * (count_x + 1)
            empty = jnp.zeros(velocity.shape[2:], jnp.float32)
            mask[rim] = jnp.zeros(velocity.shape[2:], jnp.int32)
            for k in range(3):
                velocity[k, rim] = empty
                stream[k, rim] = empty
                x_rim[side, k] = empty
    for side, there, who in z_sides:
        @pl.when(jnp.logical_not(there))
        def _():
            z_in[side] = jnp.zeros(z_in.shape[1:], jnp.float32)
            m_in[side] = jnp.zeros(m_in.shape[1:], jnp.float32)
    total[...] = jnp.zeros_like(total)
    for fetch in fetches[:4]:
        fetch.wait()

    def remote(a, b, send, recv, who):
        return pltpu.make_async_remote_copy(
            src_ref=a, dst_ref=b, send_sem=send, recv_sem=recv, device_id=who, device_id_type=MESH
        )

    def faces(side, who):
        own, rim = 1 + side * (count_x - 1), (1 - side) * (count_x + 1)
        return [
            remote(a, b, face_send.at[side, i], face_recv.at[1 - side, i], who)
            for i, (a, b) in enumerate((
                (velocity.at[:, own], velocity.at[:, rim]),
                (mask.at[own], mask.at[rim]),
                (stream.at[:, own], stream.at[:, rim]),
            ))
        ]

    def z_face(side, who):
        return [remote(z_out, z_in.at[1 - side], z_send.at[side], z_recv.at[1 - side], who)]

    def m_face(side, who):
        own = 1 + side * (count_x - 1)
        return [remote(middle.at[:, own], x_rim.at[1 - side], mx_send.at[side], mx_recv.at[1 - side], who)]

    def mz_face(side, who):
        return [remote(m_out, m_in.at[1 - side], mz_send.at[side], mz_recv.at[1 - side], who)]

    def start(make, ways):
        for side, there, who in ways:
            @pl.when(there)
            def _():
                for copy in make(side, who):
                    copy.start()

    def finish(make, ways, sent):
        for side, there, who in ways:
            @pl.when(there)
            def _():
                for copy in make(side if sent else 1 - side, who):
                    if sent:
                        copy.wait_send()
                    else:
                        copy.wait_recv()

    def send_faces():
        for fetch in fetches[4:]:
            fetch.wait()
        pl.semaphore_wait(barrier, patches - 1 + (g > 0).astype(jnp.int32) + (g < groups - 1).astype(jnp.int32))

    route(strength, fraction, cell, target, outgoing, lambda: None)
    send_faces()

    def peer(i):
        return i + (i >= p).astype(jnp.int32)

    def going(i):
        other = peer(i)
        return remote(outgoing.at[other, pl.ds(0, 7)], arrived.at[p, pl.ds(0, 7)], send_sem.at[i], recv_sem.at[p], {"patch": other})

    def coming(i):
        other = peer(i)
        return remote(outgoing.at[other, pl.ds(0, 7)], arrived.at[other, pl.ds(0, 7)], send_sem.at[i], recv_sem.at[other], {"patch": other})

    def send(i, carry):
        going(i).start()
        return carry

    lax.fori_loop(0, patches - 1, send, 0)
    start(faces, x_sides)
    pack_faces(velocity, mask, stream, z_out)
    start(z_face, z_sides)
    deposit([outgoing[p]], total, shape)

    def take_some(first, count):
        for i in range(count):
            coming(first + i).wait_recv()
        deposit([arrived[peer(first + i)] for i in range(count)], total, shape)

    def take(i, carry):
        take_some(i * GROUP, GROUP)
        return carry

    early = EARLY
    lax.fori_loop(0, early, take, 0)
    finish(z_face, z_sides, False)
    prepare(velocity, mask, stream, z_in, slope, vorticity, middle, range(1, count_x - 1))
    lax.fori_loop(early, (patches - 1) // GROUP, take, 0)
    finish(faces, x_sides, False)
    prepare(velocity, mask, stream, z_in, slope, vorticity, middle, (0, count_x - 1))
    for x in (0, count_x - 1):
        swirl(total, slope, vorticity, middle, x)
    start(m_face, x_sides)
    for x in range(1, count_x - 1):
        swirl(total, slope, vorticity, middle, x)
    pack_stream(middle, m_out)
    start(mz_face, z_sides)
    second_sweep(middle, vorticity, result)

    def sent(i, carry):
        going(i).wait_send()
        return carry

    lax.fori_loop(0, patches - 1, sent, 0)
    finish(faces, x_sides, True)
    finish(z_face, z_sides, True)
    finish(m_face, x_sides, True)
    finish(mz_face, z_sides, True)
    finish(m_face, x_sides, False)
    finish(mz_face, z_sides, False)


GROUP = 3
EARLY = 0


def write_out(vorticity, inner, x_rim, m_in, vorticity_out, result_out, result, sem):
    _, count_x, count_y, count_z = inner.shape
    written = pltpu.make_async_copy(vorticity, vorticity_out, sem.at[0])
    written.start()
    at = iota((count_y, count_z), 1)
    rim = (at == 0) | (at == count_z - 1)
    joined = join_edges(m_in[0], m_in[1])
    for k in range(3):
        for x in range(count_x):
            extra = jnp.where(rim, edge_of(joined, k * count_x + x), 0.0)
            if x == 0:
                extra = extra + x_rim[0, k]
            if x == count_x - 1:
                extra = extra + x_rim[1, k]
            result[k, x] = inner[k, x] + extra * (1.0 / 6.0)
    solved = pltpu.make_async_copy(result, result_out, sem.at[1])
    solved.start()
    written.wait()
    solved.wait()


def shards(strength, fraction, cell, patch_of, velocity, body_mask, stream_prev):
    rows = patch_of.shape[0]
    patches = lax.axis_size("patch")
    capacity = 2 * rows // patches
    parts, count_x, count_y, count_z = velocity.shape
    plane = (count_y, count_z)
    room = lambda *shape: pltpu.VMEM(shape, jnp.float32)
    ints = lambda *shape: pltpu.VMEM(shape, jnp.int32)
    dma = lambda *shape: pltpu.SemaphoreType.DMA(shape)
    whole = velocity.shape
    taken = (strength, fraction, cell.reshape(1, rows), patch_of.reshape(1, rows), velocity, body_mask, stream_prev)
    made = pl.pallas_call(
        step,
        out_shape=[room(*whole), room(*whole), room(2, parts, *plane), room(2, *plane)],
        in_specs=[HBM] * 7,
        out_specs=[VMEM] * 4,
        scratch_shapes=[
            room(3, rows), room(3, rows), ints(1, rows), ints(1, rows),
            room(parts, count_x + 2, *plane), ints(count_x + 2, *plane), room(parts, count_x + 2, *plane),
            room(patches, ROWS, capacity), room(patches, ROWS, capacity),
            room(parts * count_x * (count_y // 2 + ROWS), 2 * count_z), room(parts, count_x + 2, *plane),
            room(3, *whole),
            room(*plane), room(2, *plane), room(*plane),
            dma(7), dma(patches), dma(patches), dma(2, 3), dma(2, 3),
            dma(2), dma(2), dma(2), dma(2), dma(2), dma(2),
        ],
        compiler_params=pltpu.CompilerParams(
            collective_id=0, has_side_effects=True, vmem_limit_bytes=50 * 2**20
        ),
    )(*[pltpu.with_memory_space_constraint(array, pltpu.HBM) for array in taken])
    return tuple(pl.pallas_call(
        write_out,
        out_shape=[jax.ShapeDtypeStruct(whole, jnp.float32)] * 2,
        in_specs=[VMEM] * 4,
        out_specs=[HBM] * 2,
        scratch_shapes=[room(*whole), dma(2)],
    )(*[pltpu.with_memory_space_constraint(array, pltpu.VMEM) for array in made]))


def solution(mesh):
    in_specs = (
        P(None, ("grp", "patch")),
        P(None, ("grp", "patch")),
        P(("grp", "patch")),
        P(("grp", "patch"), None),
        P(None, "patch", None, "grp"),
        P("patch", None, "grp"),
        P(None, "patch", None, "grp"),
    )
    out_specs = (P(None, "patch", None, "grp"), P(None, "patch", None, "grp"))
    return jax.shard_map(shards, mesh=mesh, in_specs=in_specs, out_specs=out_specs, check_vma=False)
```

```python
import jax
import jax.numpy as jnp
from jax import lax
from jax.experimental import pallas as pl
from jax.experimental.pallas import tpu as pltpu
from jax.sharding import PartitionSpec as P

DT_STEP = 0.5
PEN_GAIN = 0.8
ROWS = 8
HBM = pl.BlockSpec(memory_space=pltpu.HBM)
VMEM = pl.BlockSpec(memory_space=pltpu.VMEM)
MESH = pl.DeviceIdType.MESH
NT = (((1,), (1,)), ((), ()))


def kernel(distance):
    d = jnp.minimum(jnp.abs(distance), 2.0)
    near_part = 1.0 + d * d * (1.5 * d - 2.5)
    t = 2.0 - d
    return jnp.where(d < 1.0, near_part, 0.5 * t * t * (1.0 - d))


def iota(shape, dim):
    return lax.broadcasted_iota(jnp.int32, shape, dim)


def pack_edges(planes):
    width = planes[0].shape[1]
    pair = lax.shift_right_logical(iota(planes[0].shape, 1), 1)
    packed = jnp.zeros(planes[0].shape, jnp.float32)
    for i, plane in enumerate(planes):
        packed = jnp.where(pair == i, pltpu.roll(plane, (2 * i + 1) % width, 1), packed)
    return packed


def join_edges(from_low, from_high):
    width = from_low.shape[1]
    return jnp.where(iota(from_low.shape, 1) % 2 == 0, from_low, pltpu.roll(from_high, width - 2, 1))


def edge_of(joined, i):
    width = joined.shape[1]
    return pltpu.roll(joined, width - 2 * i, 1) if i else joined


def along_z(plane, edge):
    width = plane.shape[1]
    at = iota(plane.shape, 1)
    below = jnp.where(at == 0, edge, pltpu.roll(plane, 1, 1))
    above = jnp.where(at == width - 1, edge, pltpu.roll(plane, width - 1, 1))
    return below, above


def along_y(plane):
    height = plane.shape[0]
    at = iota(plane.shape, 0)
    below = jnp.where(at == 0, 0.0, pltpu.roll(plane, 1, 0))
    above = jnp.where(at == height - 1, 0.0, pltpu.roll(plane, height - 1, 0))
    return below, above


def rank(target, patches, chunk):
    turns = target.shape[1] // chunk
    tri = (iota((chunk, chunk), 0) < iota((chunk, chunk), 1)).astype(jnp.float32).astype(jnp.bfloat16)
    chosen = [
        (iota((patches, chunk), 0) == target[:, pl.ds(turn * chunk, chunk)]).astype(jnp.float32) for turn in range(turns)
    ]
    stacked = jnp.concatenate(chosen, axis=0).astype(jnp.bfloat16)
    prefix = jnp.dot(stacked, tri, preferred_element_type=jnp.float32)
    running = jnp.zeros((patches, 1), jnp.float32)
    result = []
    for turn in range(turns):
        named = chosen[turn]
        before = prefix[turn * patches : (turn + 1) * patches] + running
        running = running + jnp.sum(named, axis=1, keepdims=True)
        result.append(jnp.sum(before * named, axis=0, keepdims=True).astype(jnp.int32))
    return result


def route(strength, fraction, cell, target, out, amid):
    rows = strength.shape[1]
    patches, _, capacity = out.shape
    chunk = min(512, rows)
    turns = rows // chunk
    places = rank(target, patches, chunk)
    for turn in range(turns):
        if turn == turns // 2:
            amid()
        at = pl.ds(turn * chunk, chunk)
        named = target[:, at]
        slots = (iota((capacity, chunk), 0) == places[turn]).astype(jnp.float32).astype(jnp.bfloat16)
        value = jnp.concatenate(
            [strength[:, at], fraction[:, at], cell[:, at].astype(jnp.float32), jnp.zeros((1, chunk), jnp.float32)],
            axis=0,
        )
        coarse = value.astype(jnp.bfloat16).astype(jnp.float32)
        fine = value - coarse
        pieces = []
        for p in range(patches):
            hit = named == p
            pieces.extend((jnp.where(hit, coarse, 0.0), jnp.where(hit, fine, 0.0)))
        left = jnp.concatenate(pieces, axis=0).astype(jnp.bfloat16)
        product = lax.dot_general(left, slots, NT, preferred_element_type=jnp.float32)
        product = product.reshape(patches, 2 * ROWS, capacity)
        moved = product[:, :ROWS] + product[:, ROWS:]
        if turn == 0:
            out[...] = moved
        else:
            out[...] += moved


def pack_faces(velocity, mask, stream, out):
    count_x = velocity.shape[1] - 2
    inner = range(1, count_x + 1)
    planes = [velocity[k, x] for k in range(3) for x in inner]
    planes.extend(-PEN_GAIN * mask[x].astype(jnp.float32) for x in inner)
    planes.extend(stream[k, x] for k in range(3) for x in inner)
    out[...] = pack_edges(planes)


def spread(pattern, group, count):
    low, high = pattern[:ROWS], pattern[ROWS:]
    hits = [group == at for at in range(count)]
    result = []
    for at in range(count):
        piece = jnp.where(hits[at], low, 0.0)
        result.append(jnp.where(hits[at - 1], high, piece) if at else piece)
    return result


def deposit_operands(data, shape):
    count_x, count_y, count_z = shape
    span_y, span_z = count_y - 3, count_z - 3
    half = count_y // 2
    slots = data.shape[1]
    cell = data[6:7]
    quot_x = ((cell + 0.5) * (1.0 / (span_y * span_z))).astype(jnp.int32).astype(jnp.float32)
    rest = cell - quot_x * (span_y * span_z)
    quot_y = ((rest + 0.5) * (1.0 / span_z)).astype(jnp.int32)
    quot_z = (rest - quot_y.astype(jnp.float32) * span_z).astype(jnp.int32)
    upper = quot_y >= half
    quot_y = jnp.where(upper, quot_y - half, quot_y)

    def pattern(quot, part):
        group = lax.shift_right_logical(quot, 3)
        first = (quot - group * ROWS).astype(jnp.float32) + 1.0
        away = iota((2 * ROWS, slots), 0).astype(jnp.float32) - first
        return group, kernel(away - part)

    weight_x = kernel((iota((count_x, slots), 0).astype(jnp.float32) - (quot_x + 1.0)) - data[3:4])
    group_y, weight_y = pattern(quot_y, data[4:5])
    group_z, weight_z = pattern(quot_z, data[5:6])
    window = jnp.concatenate(spread(weight_y, group_y, half // ROWS + 1), axis=0)
    lines = [window[y : y + 1] for y in range(half + 4)]
    depth = jnp.concatenate(spread(weight_z, group_z, count_z // ROWS), axis=0)
    depth = jnp.concatenate([jnp.where(upper, 0.0, depth), jnp.where(upper, depth, 0.0)], axis=0).astype(jnp.bfloat16)
    pieces = []
    for k in range(3):
        scaled = data[k : k + 1] * weight_x
        pieces.extend(scaled * line for line in lines)
    return jnp.concatenate(pieces, axis=0).astype(jnp.bfloat16), depth


def deposit(blocks, total, shape):
    pairs = [deposit_operands(block, shape) for block in blocks]
    left = jnp.concatenate([pair[0] for pair in pairs], axis=1)
    right = jnp.concatenate([pair[1] for pair in pairs], axis=1)
    product = lax.dot_general(left, right, NT, preferred_element_type=jnp.float32)
    count_z = shape[2]
    total[0] += product[:, :count_z]
    total[1] += product[:, count_z:]


def prepare(velocity, mask, stream, z_in, slope, curl, middle):
    _, count_x, count_y, _ = curl.shape
    joined = join_edges(z_in[0], z_in[1])
    for x in range(count_x):
        first, last = x == 0, x == count_x - 1
        own_edge = edge_of(joined, 3 * count_x + x)
        own = -PEN_GAIN * mask[x + 1].astype(jnp.float32)
        before = None if first else -PEN_GAIN * mask[x].astype(jnp.float32)
        after = None if last else -PEN_GAIN * mask[x + 2].astype(jnp.float32)
        turned = [None] * 3

        def add(k, change):
            turned[k] = change if turned[k] is None else turned[k] + change

        for k in range(3):
            plane = velocity[k, x + 1]
            under = None if first else velocity[k, x]
            over = None if last else velocity[k, x + 2]
            y_below, y_above = along_y(plane)
            lane = k * count_x + x
            edge = edge_of(joined, lane)
            z_below, z_above = along_z(plane, edge)
            slope[0, k, x] = (0.5 * DT_STEP) * (over if first else -under if last else over - under)
            slope[1, k, x] = (0.5 * DT_STEP) * (y_above - y_below)
            slope[2, k, x] = (0.5 * DT_STEP) * (z_above - z_below)
            penal = own * plane
            if k != 0:
                change = after * over if first else -(before * under) if last else after * over - before * under
                add(3 - k, change if k == 1 else -change)
            if k != 1:
                y_below, y_above = along_y(penal)
                change = y_above - y_below
                add(2 - k, change if k == 2 else -change)
            if k != 2:
                z_below, z_above = along_z(penal, own_edge * edge)
                change = z_above - z_below
                add(1 - k, change if k == 0 else -change)
            near = within_plane(stream[k, x + 1], edge_of(joined, 4 * count_x + lane))
            if not first:
                near = near + stream[k, x]
            if not last:
                near = near + stream[k, x + 2]
            middle[k, x + 1] = near * (1.0 / 6.0)
        for k in range(3):
            curl[k, x] = 0.5 * turned[k]


def add_x_faces(velocity, mask, stream, slope, curl, middle):
    count_x = curl.shape[1]
    for rim, x, sign in ((0, 0, -1.0), (count_x + 1, count_x - 1, 1.0)):
        gain = (-0.5 * sign * PEN_GAIN) * mask[rim].astype(jnp.float32)
        for k in range(3):
            face = velocity[k, rim]
            slope[0, k, x] += (0.5 * sign * DT_STEP) * face
            if k == 1:
                curl[2, x] += gain * face
            if k == 2:
                curl[1, x] -= gain * face
            middle[k, x + 1] += stream[k, rim] * (1.0 / 6.0)


def deposited(total, k, x, count_x, half):
    window = half + 4
    rows = pl.ds(k * window * count_x + x, window, count_x)
    count_z = total.shape[2]
    lower, upper = total[0, rows, :], total[1, rows, :]
    shared = jnp.concatenate([lower[half:], jnp.zeros((half - 4, count_z), jnp.float32)], axis=0)
    return jnp.concatenate([lower[:half], upper[:half] + shared], axis=0)


def swirl(total, slope, curl, middle, x):
    _, count_x, count_y, _ = curl.shape
    moved = [deposited(total, k, x, count_x, count_y // 2) for k in range(3)]
    for k in range(3):
        stretch = moved[0] * slope[0, k, x] + moved[1] * slope[1, k, x] + moved[2] * slope[2, k, x]
        value = moved[k] + stretch + curl[k, x]
        curl[k, x] = value
        middle[k, x + 1] += value * (1.0 / 6.0)


def within_plane(plane, edge):
    y_below, y_above = along_y(plane)
    z_below, z_above = along_z(plane, edge)
    return y_below + y_above + z_below + z_above


def second_sweep(middle, vorticity, result):
    _, count_x, count_y, count_z = vorticity.shape
    empty = jnp.zeros((count_y, count_z), jnp.float32)
    for k in range(3):
        for x in range(count_x):
            summed = within_plane(middle[k, x + 1], empty)
            if x > 0:
                summed = summed + middle[k, x]
            if x < count_x - 1:
                summed = summed + middle[k, x + 2]
            result[k, x] = (summed + vorticity[k, x]) * (1.0 / 6.0)


def pack_stream(stream, out):
    count_x = stream.shape[1] - 2
    out[...] = pack_edges([stream[k, x] for k in range(3) for x in range(1, count_x + 1)])


def step(
    strength_in, fraction_in, cell_in, target_in, velocity_in, mask_in, stream_in,
    vorticity, result, x_rim, m_in,
    strength, fraction, cell, target, velocity, mask, stream,
    outgoing, arrived, total, middle, slope, z_out, z_in, m_out,
    fetch_sem, send_sem, recv_sem, face_send, face_recv, z_send, z_recv, mx_send, mx_recv, mz_send, mz_recv,
):
    groups, patches = lax.axis_size("grp"), lax.axis_size("patch")
    g, p = lax.axis_index("grp"), lax.axis_index("patch")
    shape = vorticity.shape[1:]
    count_x = shape[0]
    fetches = [
        (strength_in, strength), (fraction_in, fraction), (cell_in, cell), (target_in, target),
        (velocity_in, velocity.at[:, pl.ds(1, count_x)]),
        (mask_in, mask.at[pl.ds(1, count_x)]),
        (stream_in, stream.at[:, pl.ds(1, count_x)]),
    ]
    fetches = [pltpu.make_async_copy(a, b, fetch_sem.at[i]) for i, (a, b) in enumerate(fetches)]
    for fetch in fetches:
        fetch.start()

    barrier = pltpu.get_barrier_semaphore()

    def greet(i, carry):
        pl.semaphore_signal(barrier, inc=1, device_id={"patch": lax.rem(p + i, patches)}, device_id_type=MESH)
        return carry

    lax.fori_loop(1, patches, greet, 0)
    sides = (
        (0, "patch", p, p > 0, p - 1), (1, "patch", p, p < patches - 1, p + 1),
        (0, "grp", g, g > 0, g - 1), (1, "grp", g, g < groups - 1, g + 1),
    )
    x_sides = [(side, there, {axis: who}) for side, axis, _, there, who in sides[:2]]
    z_sides = [(side, there, {axis: who}) for side, axis, _, there, who in sides[2:]]
    for side, there, who in z_sides:
        @pl.when(there)
        def _():
            pl.semaphore_signal(barrier, inc=1, device_id=who, device_id_type=MESH)

    for side, there, who in x_sides:
        @pl.when(jnp.logical_not(there))
        def _():
            rim = side * (count_x + 1)
            empty = jnp.zeros(velocity.shape[2:], jnp.float32)
            mask[rim] = jnp.zeros(velocity.shape[2:], jnp.int32)
            for k in range(3):
                velocity[k, rim] = empty
                stream[k, rim] = empty
                x_rim[side, k] = empty
    for side, there, who in z_sides:
        @pl.when(jnp.logical_not(there))
        def _():
            z_in[side] = jnp.zeros(z_in.shape[1:], jnp.float32)
            m_in[side] = jnp.zeros(m_in.shape[1:], jnp.float32)
    total[...] = jnp.zeros_like(total)
    for fetch in fetches[:4]:
        fetch.wait()

    def remote(a, b, send, recv, who):
        return pltpu.make_async_remote_copy(
            src_ref=a, dst_ref=b, send_sem=send, recv_sem=recv, device_id=who, device_id_type=MESH
        )

    def faces(side, who):
        own, rim = 1 + side * (count_x - 1), (1 - side) * (count_x + 1)
        return [
            remote(a, b, face_send.at[side, i], face_recv.at[1 - side, i], who)
            for i, (a, b) in enumerate((
                (velocity.at[:, own], velocity.at[:, rim]),
                (mask.at[own], mask.at[rim]),
                (stream.at[:, own], stream.at[:, rim]),
            ))
        ]

    def z_face(side, who):
        return [remote(z_out, z_in.at[1 - side], z_send.at[side], z_recv.at[1 - side], who)]

    def m_face(side, who):
        own = 1 + side * (count_x - 1)
        return [remote(middle.at[:, own], x_rim.at[1 - side], mx_send.at[side], mx_recv.at[1 - side], who)]

    def mz_face(side, who):
        return [remote(m_out, m_in.at[1 - side], mz_send.at[side], mz_recv.at[1 - side], who)]

    def start(make, ways):
        for side, there, who in ways:
            @pl.when(there)
            def _():
                for copy in make(side, who):
                    copy.start()

    def finish(make, ways, sent):
        for side, there, who in ways:
            @pl.when(there)
            def _():
                for copy in make(side if sent else 1 - side, who):
                    if sent:
                        copy.wait_send()
                    else:
                        copy.wait_recv()

    def send_faces():
        for fetch in fetches[4:]:
            fetch.wait()
        pl.semaphore_wait(barrier, patches - 1 + (g > 0).astype(jnp.int32) + (g < groups - 1).astype(jnp.int32))

    route(strength, fraction, cell, target, outgoing, lambda: None)
    send_faces()

    def peer(i):
        return i + (i >= p).astype(jnp.int32)

    def going(i):
        other = peer(i)
        return remote(outgoing.at[other, pl.ds(0, 7)], arrived.at[p, pl.ds(0, 7)], send_sem.at[i], recv_sem.at[p], {"patch": other})

    def coming(i):
        other = peer(i)
        return remote(outgoing.at[other, pl.ds(0, 7)], arrived.at[other, pl.ds(0, 7)], send_sem.at[i], recv_sem.at[other], {"patch": other})

    def send(i, carry):
        going(i).start()
        return carry

    lax.fori_loop(0, patches - 1, send, 0)
    start(faces, x_sides)
    pack_faces(velocity, mask, stream, z_out)
    start(z_face, z_sides)
    deposit([outgoing[p]], total, shape)

    def take_some(first, count):
        for i in range(count):
            coming(first + i).wait_recv()
        deposit([arrived[peer(first + i)] for i in range(count)], total, shape)

    def take(i, carry):
        take_some(i * GROUP, GROUP)
        return carry

    finish(z_face, z_sides, False)
    prepare(velocity, mask, stream, z_in, slope, vorticity, middle)
    groups_of, rest = (patches - 1) // GROUP, (patches - 1) % GROUP
    lax.fori_loop(0, groups_of, take, 0)
    if rest:
        take_some(groups_of * GROUP, rest)
    finish(faces, x_sides, False)
    add_x_faces(velocity, mask, stream, slope, vorticity, middle)
    for x in (0, count_x - 1):
        swirl(total, slope, vorticity, middle, x)
    start(m_face, x_sides)
    for x in range(1, count_x - 1):
        swirl(total, slope, vorticity, middle, x)
    pack_stream(middle, m_out)
    start(mz_face, z_sides)
    second_sweep(middle, vorticity, result)

    def sent(i, carry):
        going(i).wait_send()
        return carry

    lax.fori_loop(0, patches - 1, sent, 0)
    finish(faces, x_sides, True)
    finish(z_face, z_sides, True)
    finish(m_face, x_sides, True)
    finish(mz_face, z_sides, True)
    finish(m_face, x_sides, False)
    finish(mz_face, z_sides, False)


GROUP = 6


def write_out(vorticity, inner, x_rim, m_in, vorticity_out, result_out, result, sem):
    _, count_x, count_y, count_z = inner.shape
    written = pltpu.make_async_copy(vorticity, vorticity_out, sem.at[0])
    written.start()
    copies = [written]
    at = iota((count_y, count_z), 1)
    rim = (at == 0) | (at == count_z - 1)
    joined = join_edges(m_in[0], m_in[1])
    for k in range(3):
        for x in range(count_x):
            extra = jnp.where(rim, edge_of(joined, k * count_x + x), 0.0)
            if x == 0:
                extra = extra + x_rim[0, k]
            if x == count_x - 1:
                extra = extra + x_rim[1, k]
            result[k, x] = inner[k, x] + extra * (1.0 / 6.0)
        solved = pltpu.make_async_copy(result.at[k], result_out.at[k], sem.at[1 + k])
        solved.start()
        copies.append(solved)
    for copy in copies:
        copy.wait()


def shards(strength, fraction, cell, patch_of, velocity, body_mask, stream_prev):
    rows = patch_of.shape[0]
    patches = lax.axis_size("patch")
    capacity = 2 * rows // patches
    parts, count_x, count_y, count_z = velocity.shape
    plane = (count_y, count_z)
    room = lambda *shape: pltpu.VMEM(shape, jnp.float32)
    ints = lambda *shape: pltpu.VMEM(shape, jnp.int32)
    dma = lambda *shape: pltpu.SemaphoreType.DMA(shape)
    whole = velocity.shape
    taken = (strength, fraction, cell.reshape(1, rows), patch_of.reshape(1, rows), velocity, body_mask, stream_prev)
    made = pl.pallas_call(
        step,
        out_shape=[room(*whole), room(*whole), room(2, parts, *plane), room(2, *plane)],
        in_specs=[HBM] * 7,
        out_specs=[VMEM] * 4,
        scratch_shapes=[
            room(3, rows), room(3, rows), ints(1, rows), ints(1, rows),
            room(parts, count_x + 2, *plane), ints(count_x + 2, *plane), room(parts, count_x + 2, *plane),
            room(patches, ROWS, capacity), room(patches, ROWS, capacity),
            room(2, parts * count_x * (count_y // 2 + 4), count_z), room(parts, count_x + 2, *plane),
            room(3, *whole),
            room(*plane), room(2, *plane), room(*plane),
            dma(7), dma(patches), dma(patches), dma(2, 3), dma(2, 3),
            dma(2), dma(2), dma(2), dma(2), dma(2), dma(2),
        ],
        compiler_params=pltpu.CompilerParams(
            collective_id=0, has_side_effects=True, vmem_limit_bytes=50 * 2**20
        ),
    )(*[pltpu.with_memory_space_constraint(array, pltpu.HBM) for array in taken])
    return tuple(pl.pallas_call(
        write_out,
        out_shape=[jax.ShapeDtypeStruct(whole, jnp.float32)] * 2,
        in_specs=[VMEM] * 4,
        out_specs=[HBM] * 2,
        scratch_shapes=[room(*whole), dma(4)],
    )(*[pltpu.with_memory_space_constraint(array, pltpu.VMEM) for array in made]))


def solution(mesh):
    in_specs = (
        P(None, ("grp", "patch")),
        P(None, ("grp", "patch")),
        P(("grp", "patch")),
        P(("grp", "patch"), None),
        P(None, "patch", None, "grp"),
        P("patch", None, "grp"),
        P(None, "patch", None, "grp"),
    )
    out_specs = (P(None, "patch", None, "grp"), P(None, "patch", None, "grp"))
    return jax.shard_map(shards, mesh=mesh, in_specs=in_specs, out_specs=out_specs, check_vma=False)
```

```python
import jax
import jax.numpy as jnp
from jax import lax
from jax.experimental import pallas as pl
from jax.experimental.pallas import tpu as pltpu
from jax.sharding import PartitionSpec as P

DT_STEP = 0.5
PEN_GAIN = 0.8
ROWS = 8
HBM = pl.BlockSpec(memory_space=pltpu.HBM)
VMEM = pl.BlockSpec(memory_space=pltpu.VMEM)
MESH = pl.DeviceIdType.MESH
NT = (((1,), (1,)), ((), ()))


def kernel(distance):
    d = jnp.minimum(jnp.abs(distance), 2.0)
    near_part = 1.0 + d * d * (1.5 * d - 2.5)
    t = 2.0 - d
    return jnp.where(d < 1.0, near_part, 0.5 * t * t * (1.0 - d))


def iota(shape, dim):
    return lax.broadcasted_iota(jnp.int32, shape, dim)


def pack_edges(planes):
    width = planes[0].shape[1]
    pair = lax.shift_right_logical(iota(planes[0].shape, 1), 1)
    packed = jnp.zeros(planes[0].shape, jnp.float32)
    for i, plane in enumerate(planes):
        packed = jnp.where(pair == i, pltpu.roll(plane, (2 * i + 1) % width, 1), packed)
    return packed


def join_edges(from_low, from_high):
    width = from_low.shape[1]
    return jnp.where(iota(from_low.shape, 1) % 2 == 0, from_low, pltpu.roll(from_high, width - 2, 1))


def edge_of(joined, i):
    width = joined.shape[1]
    return pltpu.roll(joined, width - 2 * i, 1) if i else joined


def along_z(plane, edge):
    width = plane.shape[1]
    at = iota(plane.shape, 1)
    below = jnp.where(at == 0, edge, pltpu.roll(plane, 1, 1))
    above = jnp.where(at == width - 1, edge, pltpu.roll(plane, width - 1, 1))
    return below, above


def along_y(plane):
    height = plane.shape[0]
    at = iota(plane.shape, 0)
    below = jnp.where(at == 0, 0.0, pltpu.roll(plane, 1, 0))
    above = jnp.where(at == height - 1, 0.0, pltpu.roll(plane, height - 1, 0))
    return below, above


def rank(target, patches, chunk):
    turns = target.shape[1] // chunk
    tri = (iota((chunk, chunk), 0) < iota((chunk, chunk), 1)).astype(jnp.float32).astype(jnp.bfloat16)
    chosen = [
        (iota((patches, chunk), 0) == target[:, pl.ds(turn * chunk, chunk)]).astype(jnp.float32) for turn in range(turns)
    ]
    stacked = jnp.concatenate(chosen, axis=0).astype(jnp.bfloat16)
    prefix = jnp.dot(stacked, tri, preferred_element_type=jnp.float32)
    running = jnp.zeros((patches, 1), jnp.float32)
    result = []
    for turn in range(turns):
        named = chosen[turn]
        before = prefix[turn * patches : (turn + 1) * patches] + running
        running = running + jnp.sum(named, axis=1, keepdims=True)
        result.append(jnp.sum(before * named, axis=0, keepdims=True).astype(jnp.int32))
    return result


def route(strength, fraction, cell, target, out, amid):
    rows = strength.shape[1]
    patches, _, capacity = out.shape
    chunk = min(512, rows)
    turns = rows // chunk
    places = rank(target, patches, chunk)
    for turn in range(turns):
        if turn == turns // 2:
            amid()
        at = pl.ds(turn * chunk, chunk)
        named = target[:, at]
        slots = (iota((capacity, chunk), 0) == places[turn]).astype(jnp.float32).astype(jnp.bfloat16)
        value = jnp.concatenate(
            [strength[:, at], fraction[:, at], cell[:, at].astype(jnp.float32), jnp.zeros((1, chunk), jnp.float32)],
            axis=0,
        )
        coarse = value.astype(jnp.bfloat16).astype(jnp.float32)
        fine = value - coarse
        pieces = []
        for p in range(patches):
            hit = named == p
            pieces.extend((jnp.where(hit, coarse, 0.0), jnp.where(hit, fine, 0.0)))
        left = jnp.concatenate(pieces, axis=0).astype(jnp.bfloat16)
        product = lax.dot_general(left, slots, NT, preferred_element_type=jnp.float32)
        product = product.reshape(patches, 2 * ROWS, capacity)
        moved = product[:, :ROWS] + product[:, ROWS:]
        if turn == 0:
            out[...] = moved
        else:
            out[...] += moved


def pack_faces(velocity, mask, stream, out):
    count_x = velocity.shape[1] - 2
    inner = range(1, count_x + 1)
    planes = [velocity[k, x] for k in range(3) for x in inner]
    planes.extend(-PEN_GAIN * mask[x].astype(jnp.float32) for x in inner)
    planes.extend(stream[k, x] for k in range(3) for x in inner)
    out[...] = pack_edges(planes)


def spread(pattern, group, count):
    low, high = pattern[:ROWS], pattern[ROWS:]
    hits = [group == at for at in range(count)]
    result = []
    for at in range(count):
        piece = jnp.where(hits[at], low, 0.0)
        result.append(jnp.where(hits[at - 1], high, piece) if at else piece)
    return result


def deposit_operands(data, shape):
    count_x, count_y, count_z = shape
    span_y, span_z = count_y - 3, count_z - 3
    half = count_y // 2
    slots = data.shape[1]
    cell = data[6:7]
    quot_x = ((cell + 0.5) * (1.0 / (span_y * span_z))).astype(jnp.int32).astype(jnp.float32)
    rest = cell - quot_x * (span_y * span_z)
    quot_y = ((rest + 0.5) * (1.0 / span_z)).astype(jnp.int32)
    quot_z = (rest - quot_y.astype(jnp.float32) * span_z).astype(jnp.int32)
    upper = quot_y >= half
    quot_y = jnp.where(upper, quot_y - half, quot_y)

    def pattern(quot, part):
        group = lax.shift_right_logical(quot, 3)
        first = (quot - group * ROWS).astype(jnp.float32) + 1.0
        away = iota((2 * ROWS, slots), 0).astype(jnp.float32) - first
        return group, kernel(away - part)

    weight_x = kernel((iota((count_x, slots), 0).astype(jnp.float32) - (quot_x + 1.0)) - data[3:4])
    group_y, weight_y = pattern(quot_y, data[4:5])
    group_z, weight_z = pattern(quot_z, data[5:6])
    window = jnp.concatenate(spread(weight_y, group_y, half // ROWS + 1), axis=0)
    lines = [window[y : y + 1] for y in range(half + 4)]
    depth = jnp.concatenate(spread(weight_z, group_z, count_z // ROWS), axis=0)
    depth = jnp.concatenate([jnp.where(upper, 0.0, depth), jnp.where(upper, depth, 0.0)], axis=0).astype(jnp.bfloat16)
    pieces = []
    for k in range(3):
        scaled = data[k : k + 1] * weight_x
        pieces.extend(scaled * line for line in lines)
    return jnp.concatenate(pieces, axis=0).astype(jnp.bfloat16), depth


def deposit(blocks, total, shape):
    pairs = [deposit_operands(block, shape) for block in blocks]
    left = jnp.concatenate([pair[0] for pair in pairs], axis=1)
    right = jnp.concatenate([pair[1] for pair in pairs], axis=1)
    product = lax.dot_general(left, right, NT, preferred_element_type=jnp.float32)
    count_z = shape[2]
    total[0] += product[:, :count_z]
    total[1] += product[:, count_z:]


def prepare(velocity, mask, stream, z_in, slope, curl, middle):
    _, count_x, count_y, _ = curl.shape
    joined = join_edges(z_in[0], z_in[1])
    for x in range(count_x):
        first, last = x == 0, x == count_x - 1
        own_edge = edge_of(joined, 3 * count_x + x)
        own = -PEN_GAIN * mask[x + 1].astype(jnp.float32)
        before = None if first else -PEN_GAIN * mask[x].astype(jnp.float32)
        after = None if last else -PEN_GAIN * mask[x + 2].astype(jnp.float32)
        turned = [None] * 3

        def add(k, change):
            turned[k] = change if turned[k] is None else turned[k] + change

        for k in range(3):
            plane = velocity[k, x + 1]
            under = None if first else velocity[k, x]
            over = None if last else velocity[k, x + 2]
            y_below, y_above = along_y(plane)
            lane = k * count_x + x
            edge = edge_of(joined, lane)
            z_below, z_above = along_z(plane, edge)
            slope[0, k, x] = (0.5 * DT_STEP) * (over if first else -under if last else over - under)
            slope[1, k, x] = (0.5 * DT_STEP) * (y_above - y_below)
            slope[2, k, x] = (0.5 * DT_STEP) * (z_above - z_below)
            penal = own * plane
            if k != 0:
                change = after * over if first else -(before * under) if last else after * over - before * under
                add(3 - k, change if k == 1 else -change)
            if k != 1:
                y_below, y_above = along_y(penal)
                change = y_above - y_below
                add(2 - k, change if k == 2 else -change)
            if k != 2:
                z_below, z_above = along_z(penal, own_edge * edge)
                change = z_above - z_below
                add(1 - k, change if k == 0 else -change)
            near = within_plane(stream[k, x + 1], edge_of(joined, 4 * count_x + lane))
            if not first:
                near = near + stream[k, x]
            if not last:
                near = near + stream[k, x + 2]
            middle[k, x + 1] = near * (1.0 / 6.0)
        for k in range(3):
            curl[k, x] = 0.5 * turned[k]


def add_x_faces(velocity, mask, stream, slope, curl, middle):
    count_x = curl.shape[1]
    for rim, x, sign in ((0, 0, -1.0), (count_x + 1, count_x - 1, 1.0)):
        gain = (-0.5 * sign * PEN_GAIN) * mask[rim].astype(jnp.float32)
        for k in range(3):
            face = velocity[k, rim]
            slope[0, k, x] += (0.5 * sign * DT_STEP) * face
            if k == 1:
                curl[2, x] += gain * face
            if k == 2:
                curl[1, x] -= gain * face
            middle[k, x + 1] += stream[k, rim] * (1.0 / 6.0)


def deposited(total, k, x, count_x, half):
    window = half + 4
    rows = pl.ds(k * window * count_x + x, window, count_x)
    count_z = total.shape[2]
    lower, upper = total[0, rows, :], total[1, rows, :]
    shared = jnp.concatenate([lower[half:], jnp.zeros((half - 4, count_z), jnp.float32)], axis=0)
    return jnp.concatenate([lower[:half], upper[:half] + shared], axis=0)


def swirl(total, slope, curl, middle, x):
    _, count_x, count_y, _ = curl.shape
    moved = [deposited(total, k, x, count_x, count_y // 2) for k in range(3)]
    for k in range(3):
        stretch = moved[0] * slope[0, k, x] + moved[1] * slope[1, k, x] + moved[2] * slope[2, k, x]
        value = moved[k] + stretch + curl[k, x]
        curl[k, x] = value
        middle[k, x + 1] += value * (1.0 / 6.0)


def within_plane(plane, edge):
    y_below, y_above = along_y(plane)
    z_below, z_above = along_z(plane, edge)
    return y_below + y_above + z_below + z_above


def second_sweep(middle, vorticity, result):
    _, count_x, count_y, count_z = vorticity.shape
    empty = jnp.zeros((count_y, count_z), jnp.float32)
    for k in range(3):
        for x in range(count_x):
            summed = within_plane(middle[k, x + 1], empty)
            if x > 0:
                summed = summed + middle[k, x]
            if x < count_x - 1:
                summed = summed + middle[k, x + 2]
            result[k, x] = (summed + vorticity[k, x]) * (1.0 / 6.0)


def pack_stream(stream, out):
    count_x = stream.shape[1] - 2
    out[...] = pack_edges([stream[k, x] for k in range(3) for x in range(1, count_x + 1)])


def step(
    strength_in, fraction_in, cell_in, target_in, velocity_in, mask_in, stream_in,
    vorticity, result, x_rim, m_in,
    strength, fraction, cell, target, velocity, mask, stream,
    outgoing, arrived, total, middle, slope, z_out, z_in, m_out,
    fetch_sem, send_sem, recv_sem, face_send, face_recv, z_send, z_recv, mx_send, mx_recv, mz_send, mz_recv,
):
    groups, patches = lax.axis_size("grp"), lax.axis_size("patch")
    g, p = lax.axis_index("grp"), lax.axis_index("patch")
    shape = vorticity.shape[1:]
    count_x = shape[0]
    fetches = [
        (strength_in, strength), (fraction_in, fraction), (cell_in, cell), (target_in, target),
        (velocity_in, velocity.at[:, pl.ds(1, count_x)]),
        (mask_in, mask.at[pl.ds(1, count_x)]),
        (stream_in, stream.at[:, pl.ds(1, count_x)]),
    ]
    fetches = [pltpu.make_async_copy(a, b, fetch_sem.at[i]) for i, (a, b) in enumerate(fetches)]
    for fetch in fetches:
        fetch.start()

    barrier = pltpu.get_barrier_semaphore()

    def greet(i, carry):
        pl.semaphore_signal(barrier, inc=1, device_id={"patch": lax.rem(p + i, patches)}, device_id_type=MESH)
        return carry

    lax.fori_loop(1, patches, greet, 0)
    sides = (
        (0, "patch", p, p > 0, p - 1), (1, "patch", p, p < patches - 1, p + 1),
        (0, "grp", g, g > 0, g - 1), (1, "grp", g, g < groups - 1, g + 1),
    )
    x_sides = [(side, there, {axis: who}) for side, axis, _, there, who in sides[:2]]
    z_sides = [(side, there, {axis: who}) for side, axis, _, there, who in sides[2:]]
    for side, there, who in z_sides:
        @pl.when(there)
        def _():
            pl.semaphore_signal(barrier, inc=1, device_id=who, device_id_type=MESH)

    for side, there, who in x_sides:
        @pl.when(jnp.logical_not(there))
        def _():
            rim = side * (count_x + 1)
            empty = jnp.zeros(velocity.shape[2:], jnp.float32)
            mask[rim] = jnp.zeros(velocity.shape[2:], jnp.int32)
            for k in range(3):
                velocity[k, rim] = empty
                stream[k, rim] = empty
                x_rim[side, k] = empty
    for side, there, who in z_sides:
        @pl.when(jnp.logical_not(there))
        def _():
            z_in[side] = jnp.zeros(z_in.shape[1:], jnp.float32)
            m_in[side] = jnp.zeros(m_in.shape[1:], jnp.float32)
    total[...] = jnp.zeros_like(total)
    for fetch in fetches[:4]:
        fetch.wait()

    def remote(a, b, send, recv, who):
        return pltpu.make_async_remote_copy(
            src_ref=a, dst_ref=b, send_sem=send, recv_sem=recv, device_id=who, device_id_type=MESH
        )

    def faces(side, who):
        own, rim = 1 + side * (count_x - 1), (1 - side) * (count_x + 1)
        return [
            remote(a, b, face_send.at[side, i], face_recv.at[1 - side, i], who)
            for i, (a, b) in enumerate((
                (velocity.at[:, own], velocity.at[:, rim]),
                (mask.at[own], mask.at[rim]),
                (stream.at[:, own], stream.at[:, rim]),
            ))
        ]

    def z_face(side, who):
        return [remote(z_out, z_in.at[1 - side], z_send.at[side], z_recv.at[1 - side], who)]

    def m_face(side, who):
        own = 1 + side * (count_x - 1)
        return [remote(middle.at[:, own], x_rim.at[1 - side], mx_send.at[side], mx_recv.at[1 - side], who)]

    def mz_face(side, who):
        return [remote(m_out, m_in.at[1 - side], mz_send.at[side], mz_recv.at[1 - side], who)]

    def start(make, ways):
        for side, there, who in ways:
            @pl.when(there)
            def _():
                for copy in make(side, who):
                    copy.start()

    def finish(make, ways, sent):
        for side, there, who in ways:
            @pl.when(there)
            def _():
                for copy in make(side if sent else 1 - side, who):
                    if sent:
                        copy.wait_send()
                    else:
                        copy.wait_recv()

    def send_faces():
        pl.semaphore_wait(barrier, patches - 1 + (g > 0).astype(jnp.int32) + (g < groups - 1).astype(jnp.int32))

    route(strength, fraction, cell, target, outgoing, lambda: None)
    for fetch in fetches[4:]:
        fetch.wait()
    pack_faces(velocity, mask, stream, z_out)
    send_faces()

    def peer(i):
        return i + (i >= p).astype(jnp.int32)

    def going(i):
        other = peer(i)
        return remote(outgoing.at[other, pl.ds(0, 7)], arrived.at[p, pl.ds(0, 7)], send_sem.at[i], recv_sem.at[p], {"patch": other})

    def coming(i):
        other = peer(i)
        return remote(outgoing.at[other, pl.ds(0, 7)], arrived.at[other, pl.ds(0, 7)], send_sem.at[i], recv_sem.at[other], {"patch": other})

    def send(i, carry):
        going(i).start()
        return carry

    lax.fori_loop(0, patches - 1, send, 0)
    start(z_face, z_sides)
    start(faces, x_sides)
    deposit([outgoing[p]], total, shape)

    def take_some(first, count):
        for i in range(count):
            coming(first + i).wait_recv()
        deposit([arrived[peer(first + i)] for i in range(count)], total, shape)

    def take(i, carry):
        take_some(i * GROUP, GROUP)
        return carry

    finish(z_face, z_sides, False)
    prepare(velocity, mask, stream, z_in, slope, vorticity, middle)
    groups_of, rest = (patches - 1) // GROUP, (patches - 1) % GROUP
    lax.fori_loop(0, groups_of, take, 0)
    if rest:
        take_some(groups_of * GROUP, rest)
    finish(faces, x_sides, False)
    add_x_faces(velocity, mask, stream, slope, vorticity, middle)
    for x in (0, count_x - 1):
        swirl(total, slope, vorticity, middle, x)
    start(m_face, x_sides)
    for x in range(1, count_x - 1):
        swirl(total, slope, vorticity, middle, x)
    pack_stream(middle, m_out)
    start(mz_face, z_sides)
    second_sweep(middle, vorticity, result)

    def sent(i, carry):
        going(i).wait_send()
        return carry

    lax.fori_loop(0, patches - 1, sent, 0)
    finish(faces, x_sides, True)
    finish(z_face, z_sides, True)
    finish(m_face, x_sides, True)
    finish(mz_face, z_sides, True)
    finish(m_face, x_sides, False)
    finish(mz_face, z_sides, False)


GROUP = 6


def write_out(vorticity, inner, x_rim, m_in, vorticity_out, result_out, result, sem):
    _, count_x, count_y, count_z = inner.shape
    written = pltpu.make_async_copy(vorticity, vorticity_out, sem.at[0])
    written.start()
    copies = [written]
    at = iota((count_y, count_z), 1)
    rim = (at == 0) | (at == count_z - 1)
    joined = join_edges(m_in[0], m_in[1])
    for k in range(3):
        for x in range(count_x):
            extra = jnp.where(rim, edge_of(joined, k * count_x + x), 0.0)
            if x == 0:
                extra = extra + x_rim[0, k]
            if x == count_x - 1:
                extra = extra + x_rim[1, k]
            result[k, x] = inner[k, x] + extra * (1.0 / 6.0)
        solved = pltpu.make_async_copy(result.at[k], result_out.at[k], sem.at[1 + k])
        solved.start()
        copies.append(solved)
    for copy in copies:
        copy.wait()


def shards(strength, fraction, cell, patch_of, velocity, body_mask, stream_prev):
    rows = patch_of.shape[0]
    patches = lax.axis_size("patch")
    capacity = 2 * rows // patches
    parts, count_x, count_y, count_z = velocity.shape
    plane = (count_y, count_z)
    room = lambda *shape: pltpu.VMEM(shape, jnp.float32)
    ints = lambda *shape: pltpu.VMEM(shape, jnp.int32)
    dma = lambda *shape: pltpu.SemaphoreType.DMA(shape)
    whole = velocity.shape
    taken = (strength, fraction, cell.reshape(1, rows), patch_of.reshape(1, rows), velocity, body_mask, stream_prev)
    made = pl.pallas_call(
        step,
        out_shape=[room(*whole), room(*whole), room(2, parts, *plane), room(2, *plane)],
        in_specs=[HBM] * 7,
        out_specs=[VMEM] * 4,
        scratch_shapes=[
            room(3, rows), room(3, rows), ints(1, rows), ints(1, rows),
            room(parts, count_x + 2, *plane), ints(count_x + 2, *plane), room(parts, count_x + 2, *plane),
            room(patches, ROWS, capacity), room(patches, ROWS, capacity),
            room(2, parts * count_x * (count_y // 2 + 4), count_z), room(parts, count_x + 2, *plane),
            room(3, *whole),
            room(*plane), room(2, *plane), room(*plane),
            dma(7), dma(patches), dma(patches), dma(2, 3), dma(2, 3),
            dma(2), dma(2), dma(2), dma(2), dma(2), dma(2),
        ],
        compiler_params=pltpu.CompilerParams(
            collective_id=0, has_side_effects=True, vmem_limit_bytes=50 * 2**20
        ),
    )(*[pltpu.with_memory_space_constraint(array, pltpu.HBM) for array in taken])
    return tuple(pl.pallas_call(
        write_out,
        out_shape=[jax.ShapeDtypeStruct(whole, jnp.float32)] * 2,
        in_specs=[VMEM] * 4,
        out_specs=[HBM] * 2,
        scratch_shapes=[room(*whole), dma(4)],
    )(*[pltpu.with_memory_space_constraint(array, pltpu.VMEM) for array in made]))


def solution(mesh):
    in_specs = (
        P(None, ("grp", "patch")),
        P(None, ("grp", "patch")),
        P(("grp", "patch")),
        P(("grp", "patch"), None),
        P(None, "patch", None, "grp"),
        P("patch", None, "grp"),
        P(None, "patch", None, "grp"),
    )
    out_specs = (P(None, "patch", None, "grp"), P(None, "patch", None, "grp"))
    return jax.shard_map(shards, mesh=mesh, in_specs=in_specs, out_specs=out_specs, check_vma=False)
```

```python
import jax
import jax.numpy as jnp
from jax import lax
from jax.experimental import pallas as pl
from jax.experimental.pallas import tpu as pltpu
from jax.sharding import PartitionSpec as P

DT_STEP = 0.5
PEN_GAIN = 0.8
ROWS = 8
HBM = pl.BlockSpec(memory_space=pltpu.HBM)
VMEM = pl.BlockSpec(memory_space=pltpu.VMEM)
MESH = pl.DeviceIdType.MESH
NT = (((1,), (1,)), ((), ()))


def kernel(distance):
    d = jnp.minimum(jnp.abs(distance), 2.0)
    near_part = 1.0 + d * d * (1.5 * d - 2.5)
    t = 2.0 - d
    return jnp.where(d < 1.0, near_part, 0.5 * t * t * (1.0 - d))


def iota(shape, dim):
    return lax.broadcasted_iota(jnp.int32, shape, dim)


def pack_edges(planes):
    width = planes[0].shape[1]
    pair = lax.shift_right_logical(iota(planes[0].shape, 1), 1)
    packed = jnp.zeros(planes[0].shape, jnp.float32)
    for i, plane in enumerate(planes):
        packed = jnp.where(pair == i, pltpu.roll(plane, (2 * i + 1) % width, 1), packed)
    return packed


def join_edges(from_low, from_high):
    width = from_low.shape[1]
    return jnp.where(iota(from_low.shape, 1) % 2 == 0, from_low, pltpu.roll(from_high, width - 2, 1))


def edge_of(joined, i):
    width = joined.shape[1]
    return pltpu.roll(joined, width - 2 * i, 1) if i else joined


def along_z(plane, edge):
    width = plane.shape[1]
    at = iota(plane.shape, 1)
    below = jnp.where(at == 0, edge, pltpu.roll(plane, 1, 1))
    above = jnp.where(at == width - 1, edge, pltpu.roll(plane, width - 1, 1))
    return below, above


def along_y(plane):
    height = plane.shape[0]
    at = iota(plane.shape, 0)
    below = jnp.where(at == 0, 0.0, pltpu.roll(plane, 1, 0))
    above = jnp.where(at == height - 1, 0.0, pltpu.roll(plane, height - 1, 0))
    return below, above


def rank(target, patches, chunk):
    turns = target.shape[1] // chunk
    tri = (iota((chunk, chunk), 0) < iota((chunk, chunk), 1)).astype(jnp.float32).astype(jnp.bfloat16)
    chosen = [
        (iota((patches, chunk), 0) == target[:, pl.ds(turn * chunk, chunk)]).astype(jnp.float32) for turn in range(turns)
    ]
    stacked = jnp.concatenate(chosen, axis=0).astype(jnp.bfloat16)
    prefix = jnp.dot(stacked, tri, preferred_element_type=jnp.float32)
    running = jnp.zeros((patches, 1), jnp.float32)
    result = []
    for turn in range(turns):
        named = chosen[turn]
        before = prefix[turn * patches : (turn + 1) * patches] + running
        running = running + jnp.sum(named, axis=1, keepdims=True)
        result.append(jnp.sum(before * named, axis=0, keepdims=True).astype(jnp.int32))
    return result


def route(strength, fraction, cell, target, out, amid):
    rows = strength.shape[1]
    patches, _, capacity = out.shape
    chunk = min(512, rows)
    turns = rows // chunk
    places = rank(target, patches, chunk)
    for turn in range(turns):
        if turn == turns // 2:
            amid()
        at = pl.ds(turn * chunk, chunk)
        named = target[:, at]
        slots = (iota((capacity, chunk), 0) == places[turn]).astype(jnp.float32).astype(jnp.bfloat16)
        value = jnp.concatenate(
            [strength[:, at], fraction[:, at], cell[:, at].astype(jnp.float32), jnp.zeros((1, chunk), jnp.float32)],
            axis=0,
        )
        coarse = value.astype(jnp.bfloat16).astype(jnp.float32)
        fine = value - coarse
        pieces = []
        for p in range(patches):
            hit = named == p
            pieces.extend((jnp.where(hit, coarse, 0.0), jnp.where(hit, fine, 0.0)))
        left = jnp.concatenate(pieces, axis=0).astype(jnp.bfloat16)
        product = lax.dot_general(left, slots, NT, preferred_element_type=jnp.float32)
        product = product.reshape(patches, 2 * ROWS, capacity)
        moved = product[:, :ROWS] + product[:, ROWS:]
        if turn == 0:
            out[...] = moved
        else:
            out[...] += moved


def pack_faces(velocity, mask, stream, out):
    count_x = velocity.shape[1] - 2
    inner = range(1, count_x + 1)
    planes = [velocity[k, x] for k in range(3) for x in inner]
    planes.extend(-PEN_GAIN * mask[x].astype(jnp.float32) for x in inner)
    planes.extend(stream[k, x] for k in range(3) for x in inner)
    out[...] = pack_edges(planes)


def spread(pattern, group, count):
    low, high = pattern[:ROWS], pattern[ROWS:]
    hits = [group == at for at in range(count)]
    result = []
    for at in range(count):
        piece = jnp.where(hits[at], low, 0.0)
        result.append(jnp.where(hits[at - 1], high, piece) if at else piece)
    return result


def deposit_operands(data, shape):
    count_x, count_y, count_z = shape
    span_y, span_z = count_y - 3, count_z - 3
    half = count_y // 2
    slots = data.shape[1]
    cell = data[6:7]
    quot_x = ((cell + 0.5) * (1.0 / (span_y * span_z))).astype(jnp.int32).astype(jnp.float32)
    rest = cell - quot_x * (span_y * span_z)
    quot_y = ((rest + 0.5) * (1.0 / span_z)).astype(jnp.int32)
    quot_z = (rest - quot_y.astype(jnp.float32) * span_z).astype(jnp.int32)
    upper = quot_y >= half
    quot_y = jnp.where(upper, quot_y - half, quot_y)

    def pattern(quot, part):
        group = lax.shift_right_logical(quot, 3)
        first = (quot - group * ROWS).astype(jnp.float32) + 1.0
        away = iota((2 * ROWS, slots), 0).astype(jnp.float32) - first
        return group, kernel(away - part)

    weight_x = kernel((iota((count_x, slots), 0).astype(jnp.float32) - (quot_x + 1.0)) - data[3:4])
    group_y, weight_y = pattern(quot_y, data[4:5])
    group_z, weight_z = pattern(quot_z, data[5:6])
    window = jnp.concatenate(spread(weight_y, group_y, half // ROWS + 1), axis=0)
    lines = [window[y : y + 1] for y in range(half + 4)]
    depth = jnp.concatenate(spread(weight_z, group_z, count_z // ROWS), axis=0)
    depth = jnp.concatenate([jnp.where(upper, 0.0, depth), jnp.where(upper, depth, 0.0)], axis=0).astype(jnp.bfloat16)
    pieces = []
    for k in range(3):
        scaled = data[k : k + 1] * weight_x
        pieces.extend(scaled * line for line in lines)
    return jnp.concatenate(pieces, axis=0).astype(jnp.bfloat16), depth


def deposit(blocks, total, shape):
    pairs = [deposit_operands(block, shape) for block in blocks]
    left = jnp.concatenate([pair[0] for pair in pairs], axis=1)
    right = jnp.concatenate([pair[1] for pair in pairs], axis=1)
    product = lax.dot_general(left, right, NT, preferred_element_type=jnp.float32)
    count_z = shape[2]
    total[0] += product[:, :count_z]
    total[1] += product[:, count_z:]


def prepare(velocity, mask, stream, z_in, slope, curl, middle):
    _, count_x, count_y, _ = curl.shape
    joined = join_edges(z_in[0], z_in[1])
    for x in range(count_x):
        first, last = x == 0, x == count_x - 1
        own_edge = edge_of(joined, 3 * count_x + x)
        own = -PEN_GAIN * mask[x + 1].astype(jnp.float32)
        before = None if first else -PEN_GAIN * mask[x].astype(jnp.float32)
        after = None if last else -PEN_GAIN * mask[x + 2].astype(jnp.float32)
        turned = [None] * 3

        def add(k, change):
            turned[k] = change if turned[k] is None else turned[k] + change

        for k in range(3):
            plane = velocity[k, x + 1]
            under = None if first else velocity[k, x]
            over = None if last else velocity[k, x + 2]
            y_below, y_above = along_y(plane)
            lane = k * count_x + x
            edge = edge_of(joined, lane)
            z_below, z_above = along_z(plane, edge)
            slope[0, k, x] = (0.5 * DT_STEP) * (over if first else -under if last else over - under)
            slope[1, k, x] = (0.5 * DT_STEP) * (y_above - y_below)
            slope[2, k, x] = (0.5 * DT_STEP) * (z_above - z_below)
            penal = own * plane
            if k != 0:
                change = after * over if first else -(before * under) if last else after * over - before * under
                add(3 - k, change if k == 1 else -change)
            if k != 1:
                y_below, y_above = along_y(penal)
                change = y_above - y_below
                add(2 - k, change if k == 2 else -change)
            if k != 2:
                z_below, z_above = along_z(penal, own_edge * edge)
                change = z_above - z_below
                add(1 - k, change if k == 0 else -change)
            near = within_plane(stream[k, x + 1], edge_of(joined, 4 * count_x + lane))
            if not first:
                near = near + stream[k, x]
            if not last:
                near = near + stream[k, x + 2]
            middle[k, x + 1] = near * (1.0 / 6.0)
        for k in range(3):
            curl[k, x] = 0.5 * turned[k]


def add_x_faces(velocity, mask, stream, slope, curl, middle):
    count_x = curl.shape[1]
    for rim, x, sign in ((0, 0, -1.0), (count_x + 1, count_x - 1, 1.0)):
        gain = (-0.5 * sign * PEN_GAIN) * mask[rim].astype(jnp.float32)
        for k in range(3):
            face = velocity[k, rim]
            slope[0, k, x] += (0.5 * sign * DT_STEP) * face
            if k == 1:
                curl[2, x] += gain * face
            if k == 2:
                curl[1, x] -= gain * face
            middle[k, x + 1] += stream[k, rim] * (1.0 / 6.0)


def deposited(total, k, x, count_x, half):
    window = half + 4
    rows = pl.ds(k * window * count_x + x, window, count_x)
    count_z = total.shape[2]
    lower, upper = total[0, rows, :], total[1, rows, :]
    shared = jnp.concatenate([lower[half:], jnp.zeros((half - 4, count_z), jnp.float32)], axis=0)
    return jnp.concatenate([lower[:half], upper[:half] + shared], axis=0)


def swirl(total, slope, curl, middle, x):
    _, count_x, count_y, _ = curl.shape
    moved = [deposited(total, k, x, count_x, count_y // 2) for k in range(3)]
    for k in range(3):
        stretch = moved[0] * slope[0, k, x] + moved[1] * slope[1, k, x] + moved[2] * slope[2, k, x]
        value = moved[k] + stretch + curl[k, x]
        curl[k, x] = value
        middle[k, x + 1] += value * (1.0 / 6.0)


def within_plane(plane, edge):
    y_below, y_above = along_y(plane)
    z_below, z_above = along_z(plane, edge)
    return y_below + y_above + z_below + z_above


def second_sweep(middle, vorticity, result):
    _, count_x, count_y, count_z = vorticity.shape
    empty = jnp.zeros((count_y, count_z), jnp.float32)
    for k in range(3):
        for x in range(count_x):
            summed = within_plane(middle[k, x + 1], empty)
            if x > 0:
                summed = summed + middle[k, x]
            if x < count_x - 1:
                summed = summed + middle[k, x + 2]
            result[k, x] = (summed + vorticity[k, x]) * (1.0 / 6.0)


def pack_stream(stream, out):
    count_x = stream.shape[1] - 2
    out[...] = pack_edges([stream[k, x] for k in range(3) for x in range(1, count_x + 1)])


def step(
    strength_in, fraction_in, cell_in, target_in, velocity_in, mask_in, stream_in,
    vorticity, result, x_rim, m_in,
    strength, fraction, cell, target, velocity, mask, stream,
    outgoing, arrived, total, middle, slope, z_out, z_in, m_out,
    fetch_sem, send_sem, recv_sem, face_send, face_recv, z_send, z_recv, mx_send, mx_recv, mz_send, mz_recv,
):
    groups, patches = lax.axis_size("grp"), lax.axis_size("patch")
    g, p = lax.axis_index("grp"), lax.axis_index("patch")
    shape = vorticity.shape[1:]
    count_x = shape[0]
    fetches = [
        (strength_in, strength), (fraction_in, fraction), (cell_in, cell), (target_in, target),
        (velocity_in, velocity.at[:, pl.ds(1, count_x)]),
        (mask_in, mask.at[pl.ds(1, count_x)]),
        (stream_in, stream.at[:, pl.ds(1, count_x)]),
    ]
    fetches = [pltpu.make_async_copy(a, b, fetch_sem.at[i]) for i, (a, b) in enumerate(fetches)]
    for fetch in fetches:
        fetch.start()

    barrier = pltpu.get_barrier_semaphore()

    def greet(i, carry):
        pl.semaphore_signal(barrier, inc=1, device_id={"patch": lax.rem(p + i, patches)}, device_id_type=MESH)
        return carry

    lax.fori_loop(1, patches, greet, 0)
    sides = (
        (0, "patch", p, p > 0, p - 1), (1, "patch", p, p < patches - 1, p + 1),
        (0, "grp", g, g > 0, g - 1), (1, "grp", g, g < groups - 1, g + 1),
    )
    x_sides = [(side, there, {axis: who}) for side, axis, _, there, who in sides[:2]]
    z_sides = [(side, there, {axis: who}) for side, axis, _, there, who in sides[2:]]
    for side, there, who in z_sides:
        @pl.when(there)
        def _():
            pl.semaphore_signal(barrier, inc=1, device_id=who, device_id_type=MESH)

    for side, there, who in x_sides:
        @pl.when(jnp.logical_not(there))
        def _():
            rim = side * (count_x + 1)
            empty = jnp.zeros(velocity.shape[2:], jnp.float32)
            mask[rim] = jnp.zeros(velocity.shape[2:], jnp.int32)
            for k in range(3):
                velocity[k, rim] = empty
                stream[k, rim] = empty
                x_rim[side, k] = empty
    for side, there, who in z_sides:
        @pl.when(jnp.logical_not(there))
        def _():
            z_in[side] = jnp.zeros(z_in.shape[1:], jnp.float32)
            m_in[side] = jnp.zeros(m_in.shape[1:], jnp.float32)
    total[...] = jnp.zeros_like(total)
    for fetch in fetches[:4]:
        fetch.wait()

    def remote(a, b, send, recv, who):
        return pltpu.make_async_remote_copy(
            src_ref=a, dst_ref=b, send_sem=send, recv_sem=recv, device_id=who, device_id_type=MESH
        )

    def faces(side, who):
        own, rim = 1 + side * (count_x - 1), (1 - side) * (count_x + 1)
        return [
            remote(a, b, face_send.at[side, i], face_recv.at[1 - side, i], who)
            for i, (a, b) in enumerate((
                (velocity.at[:, own], velocity.at[:, rim]),
                (mask.at[own], mask.at[rim]),
                (stream.at[:, own], stream.at[:, rim]),
            ))
        ]

    def z_face(side, who):
        return [remote(z_out, z_in.at[1 - side], z_send.at[side], z_recv.at[1 - side], who)]

    def m_face(side, who):
        own = 1 + side * (count_x - 1)
        return [remote(middle.at[:, own], x_rim.at[1 - side], mx_send.at[side], mx_recv.at[1 - side], who)]

    def mz_face(side, who):
        return [remote(m_out, m_in.at[1 - side], mz_send.at[side], mz_recv.at[1 - side], who)]

    def start(make, ways):
        for side, there, who in ways:
            @pl.when(there)
            def _():
                for copy in make(side, who):
                    copy.start()

    def finish(make, ways, sent):
        for side, there, who in ways:
            @pl.when(there)
            def _():
                for copy in make(side if sent else 1 - side, who):
                    if sent:
                        copy.wait_send()
                    else:
                        copy.wait_recv()

    def send_faces():
        pl.semaphore_wait(barrier, patches - 1 + (g > 0).astype(jnp.int32) + (g < groups - 1).astype(jnp.int32))

    route(strength, fraction, cell, target, outgoing, lambda: None)
    late = p >= patches - patches // 4

    def pack():
        for fetch in fetches[4:]:
            fetch.wait()
        pack_faces(velocity, mask, stream, z_out)

    pl.when(jnp.logical_not(late))(pack)
    send_faces()

    def peer(i):
        return i + (i >= p).astype(jnp.int32)

    def going(i):
        other = peer(i)
        return remote(outgoing.at[other, pl.ds(0, 7)], arrived.at[p, pl.ds(0, 7)], send_sem.at[i], recv_sem.at[p], {"patch": other})

    def coming(i):
        other = peer(i)
        return remote(outgoing.at[other, pl.ds(0, 7)], arrived.at[other, pl.ds(0, 7)], send_sem.at[i], recv_sem.at[other], {"patch": other})

    def send(i, carry):
        going(i).start()
        return carry

    lax.fori_loop(0, patches - 1, send, 0)
    pl.when(late)(pack)
    start(z_face, z_sides)
    start(faces, x_sides)
    deposit([outgoing[p]], total, shape)

    def take_some(first, count):
        for i in range(count):
            coming(first + i).wait_recv()
        deposit([arrived[peer(first + i)] for i in range(count)], total, shape)

    def take(i, carry):
        take_some(i * GROUP, GROUP)
        return carry

    finish(z_face, z_sides, False)
    prepare(velocity, mask, stream, z_in, slope, vorticity, middle)
    groups_of, rest = (patches - 1) // GROUP, (patches - 1) % GROUP
    lax.fori_loop(0, groups_of, take, 0)
    if rest:
        take_some(groups_of * GROUP, rest)
    finish(faces, x_sides, False)
    add_x_faces(velocity, mask, stream, slope, vorticity, middle)
    for x in (0, count_x - 1):
        swirl(total, slope, vorticity, middle, x)
    start(m_face, x_sides)
    for x in range(1, count_x - 1):
        swirl(total, slope, vorticity, middle, x)
    pack_stream(middle, m_out)
    start(mz_face, z_sides)
    second_sweep(middle, vorticity, result)

    def sent(i, carry):
        going(i).wait_send()
        return carry

    lax.fori_loop(0, patches - 1, sent, 0)
    finish(faces, x_sides, True)
    finish(z_face, z_sides, True)
    finish(m_face, x_sides, True)
    finish(mz_face, z_sides, True)
    finish(m_face, x_sides, False)
    finish(mz_face, z_sides, False)


GROUP = 7


def write_out(vorticity, inner, x_rim, m_in, vorticity_out, result_out, result, sem):
    _, count_x, count_y, count_z = inner.shape
    written = pltpu.make_async_copy(vorticity, vorticity_out, sem.at[0])
    written.start()
    copies = [written]
    at = iota((count_y, count_z), 1)
    rim = (at == 0) | (at == count_z - 1)
    joined = join_edges(m_in[0], m_in[1])
    for k in range(3):
        for x in range(count_x):
            extra = jnp.where(rim, edge_of(joined, k * count_x + x), 0.0)
            if x == 0:
                extra = extra + x_rim[0, k]
            if x == count_x - 1:
                extra = extra + x_rim[1, k]
            result[k, x] = inner[k, x] + extra * (1.0 / 6.0)
        solved = pltpu.make_async_copy(result.at[k], result_out.at[k], sem.at[1 + k])
        solved.start()
        copies.append(solved)
    for copy in copies:
        copy.wait()


def shards(strength, fraction, cell, patch_of, velocity, body_mask, stream_prev):
    rows = patch_of.shape[0]
    patches = lax.axis_size("patch")
    capacity = 2 * rows // patches
    parts, count_x, count_y, count_z = velocity.shape
    plane = (count_y, count_z)
    room = lambda *shape: pltpu.VMEM(shape, jnp.float32)
    ints = lambda *shape: pltpu.VMEM(shape, jnp.int32)
    dma = lambda *shape: pltpu.SemaphoreType.DMA(shape)
    whole = velocity.shape
    taken = (strength, fraction, cell.reshape(1, rows), patch_of.reshape(1, rows), velocity, body_mask, stream_prev)
    made = pl.pallas_call(
        step,
        out_shape=[room(*whole), room(*whole), room(2, parts, *plane), room(2, *plane)],
        in_specs=[HBM] * 7,
        out_specs=[VMEM] * 4,
        scratch_shapes=[
            room(3, rows), room(3, rows), ints(1, rows), ints(1, rows),
            room(parts, count_x + 2, *plane), ints(count_x + 2, *plane), room(parts, count_x + 2, *plane),
            room(patches, ROWS, capacity), room(patches, ROWS, capacity),
            room(2, parts * count_x * (count_y // 2 + 4), count_z), room(parts, count_x + 2, *plane),
            room(3, *whole),
            room(*plane), room(2, *plane), room(*plane),
            dma(7), dma(patches), dma(patches), dma(2, 3), dma(2, 3),
            dma(2), dma(2), dma(2), dma(2), dma(2), dma(2),
        ],
        compiler_params=pltpu.CompilerParams(
            collective_id=0, has_side_effects=True, vmem_limit_bytes=50 * 2**20
        ),
    )(*[pltpu.with_memory_space_constraint(array, pltpu.HBM) for array in taken])
    return tuple(pl.pallas_call(
        write_out,
        out_shape=[jax.ShapeDtypeStruct(whole, jnp.float32)] * 2,
        in_specs=[VMEM] * 4,
        out_specs=[HBM] * 2,
        scratch_shapes=[room(*whole), dma(4)],
    )(*[pltpu.with_memory_space_constraint(array, pltpu.VMEM) for array in made]))


def solution(mesh):
    in_specs = (
        P(None, ("grp", "patch")),
        P(None, ("grp", "patch")),
        P(("grp", "patch")),
        P(("grp", "patch"), None),
        P(None, "patch", None, "grp"),
        P("patch", None, "grp"),
        P(None, "patch", None, "grp"),
    )
    out_specs = (P(None, "patch", None, "grp"), P(None, "patch", None, "grp"))
    return jax.shard_map(shards, mesh=mesh, in_specs=in_specs, out_specs=out_specs, check_vma=False)
```

```python
import jax
import jax.numpy as jnp
from jax import lax
from jax.experimental import pallas as pl
from jax.experimental.pallas import tpu as pltpu
from jax.sharding import PartitionSpec as P

DT_STEP = 0.5
PEN_GAIN = 0.8
ROWS = 8
HBM = pl.BlockSpec(memory_space=pltpu.HBM)
VMEM = pl.BlockSpec(memory_space=pltpu.VMEM)
MESH = pl.DeviceIdType.MESH
NT = (((1,), (1,)), ((), ()))


def kernel(distance):
    d = jnp.minimum(jnp.abs(distance), 2.0)
    near_part = 1.0 + d * d * (1.5 * d - 2.5)
    t = 2.0 - d
    return jnp.where(d < 1.0, near_part, 0.5 * t * t * (1.0 - d))


def iota(shape, dim):
    return lax.broadcasted_iota(jnp.int32, shape, dim)


def pack_edges(planes):
    width = planes[0].shape[1]
    pair = lax.shift_right_logical(iota(planes[0].shape, 1), 1)
    packed = jnp.zeros(planes[0].shape, jnp.float32)
    for i, plane in enumerate(planes):
        packed = jnp.where(pair == i, pltpu.roll(plane, (2 * i + 1) % width, 1), packed)
    return packed


def join_edges(from_low, from_high):
    width = from_low.shape[1]
    return jnp.where(iota(from_low.shape, 1) % 2 == 0, from_low, pltpu.roll(from_high, width - 2, 1))


def edge_of(joined, i):
    width = joined.shape[1]
    return pltpu.roll(joined, width - 2 * i, 1) if i else joined


def along_z(plane, edge):
    width = plane.shape[1]
    at = iota(plane.shape, 1)
    below = jnp.where(at == 0, edge, pltpu.roll(plane, 1, 1))
    above = jnp.where(at == width - 1, edge, pltpu.roll(plane, width - 1, 1))
    return below, above


def along_y(plane):
    height = plane.shape[0]
    at = iota(plane.shape, 0)
    below = jnp.where(at == 0, 0.0, pltpu.roll(plane, 1, 0))
    above = jnp.where(at == height - 1, 0.0, pltpu.roll(plane, height - 1, 0))
    return below, above


def rank(target, patches, chunk):
    turns = target.shape[1] // chunk
    tri = (iota((chunk, chunk), 0) < iota((chunk, chunk), 1)).astype(jnp.float32).astype(jnp.bfloat16)
    chosen = [
        (iota((patches, chunk), 0) == target[:, pl.ds(turn * chunk, chunk)]).astype(jnp.float32) for turn in range(turns)
    ]
    stacked = jnp.concatenate(chosen, axis=0).astype(jnp.bfloat16)
    prefix = jnp.dot(stacked, tri, preferred_element_type=jnp.float32)
    running = jnp.zeros((patches, 1), jnp.float32)
    result = []
    for turn in range(turns):
        named = chosen[turn]
        before = prefix[turn * patches : (turn + 1) * patches] + running
        running = running + jnp.sum(named, axis=1, keepdims=True)
        result.append(jnp.sum(before * named, axis=0, keepdims=True).astype(jnp.int32))
    return result


def route(strength, fraction, cell, target, out, amid):
    rows = strength.shape[1]
    patches, _, capacity = out.shape
    chunk = min(512, rows)
    turns = rows // chunk
    places = rank(target, patches, chunk)
    for turn in range(turns):
        if turn == turns // 2:
            amid()
        at = pl.ds(turn * chunk, chunk)
        named = target[:, at]
        slots = (iota((capacity, chunk), 0) == places[turn]).astype(jnp.float32).astype(jnp.bfloat16)
        value = jnp.concatenate(
            [strength[:, at], fraction[:, at], cell[:, at].astype(jnp.float32), jnp.zeros((1, chunk), jnp.float32)],
            axis=0,
        )
        coarse = value.astype(jnp.bfloat16).astype(jnp.float32)
        fine = value - coarse
        pieces = []
        for p in range(patches):
            hit = named == p
            pieces.extend((jnp.where(hit, coarse, 0.0), jnp.where(hit, fine, 0.0)))
        left = jnp.concatenate(pieces, axis=0).astype(jnp.bfloat16)
        product = lax.dot_general(left, slots, NT, preferred_element_type=jnp.float32)
        product = product.reshape(patches, 2 * ROWS, capacity)
        moved = product[:, :ROWS] + product[:, ROWS:]
        if turn == 0:
            out[...] = moved
        else:
            out[...] += moved


def pack_faces(velocity, mask, stream, out):
    count_x = velocity.shape[1] - 2
    inner = range(1, count_x + 1)
    planes = [velocity[k, x] for k in range(3) for x in inner]
    planes.extend(-PEN_GAIN * mask[x].astype(jnp.float32) for x in inner)
    planes.extend(stream[k, x] for k in range(3) for x in inner)
    out[...] = pack_edges(planes)


def spread(pattern, group, count):
    low, high = pattern[:ROWS], pattern[ROWS:]
    hits = [group == at for at in range(count)]
    result = []
    for at in range(count):
        piece = jnp.where(hits[at], low, 0.0)
        result.append(jnp.where(hits[at - 1], high, piece) if at else piece)
    return result


def deposit_operands(data, shape):
    count_x, count_y, count_z = shape
    span_y, span_z = count_y - 3, count_z - 3
    half = count_y // 2
    slots = data.shape[1]
    cell = data[6:7]
    quot_x = ((cell + 0.5) * (1.0 / (span_y * span_z))).astype(jnp.int32).astype(jnp.float32)
    rest = cell - quot_x * (span_y * span_z)
    quot_y = ((rest + 0.5) * (1.0 / span_z)).astype(jnp.int32)
    quot_z = (rest - quot_y.astype(jnp.float32) * span_z).astype(jnp.int32)
    upper = quot_y >= half
    quot_y = jnp.where(upper, quot_y - half, quot_y)

    def pattern(quot, part):
        group = lax.shift_right_logical(quot, 3)
        first = (quot - group * ROWS).astype(jnp.float32) + 1.0
        away = iota((2 * ROWS, slots), 0).astype(jnp.float32) - first
        return group, kernel(away - part)

    weight_x = kernel((iota((count_x, slots), 0).astype(jnp.float32) - (quot_x + 1.0)) - data[3:4])
    group_y, weight_y = pattern(quot_y, data[4:5])
    group_z, weight_z = pattern(quot_z, data[5:6])
    window = jnp.concatenate(spread(weight_y, group_y, half // ROWS + 1), axis=0)
    lines = [window[y : y + 1] for y in range(half + 4)]
    depth = jnp.concatenate(spread(weight_z, group_z, count_z // ROWS), axis=0)
    depth = jnp.concatenate([jnp.where(upper, 0.0, depth), jnp.where(upper, depth, 0.0)], axis=0).astype(jnp.bfloat16)
    pieces = []
    for k in range(3):
        scaled = data[k : k + 1] * weight_x
        pieces.extend(scaled * line for line in lines)
    return jnp.concatenate(pieces, axis=0).astype(jnp.bfloat16), depth


def deposit(blocks, total, shape):
    pairs = [deposit_operands(block, shape) for block in blocks]
    left = jnp.concatenate([pair[0] for pair in pairs], axis=1)
    right = jnp.concatenate([pair[1] for pair in pairs], axis=1)
    product = lax.dot_general(left, right, NT, preferred_element_type=jnp.float32)
    count_z = shape[2]
    total[0] += product[:, :count_z]
    total[1] += product[:, count_z:]


def prepare(velocity, mask, stream, z_in, slope, curl, middle):
    _, count_x, count_y, _ = curl.shape
    joined = join_edges(z_in[0], z_in[1])
    for x in range(count_x):
        first, last = x == 0, x == count_x - 1
        own_edge = edge_of(joined, 3 * count_x + x)
        own = -PEN_GAIN * mask[x + 1].astype(jnp.float32)
        before = None if first else -PEN_GAIN * mask[x].astype(jnp.float32)
        after = None if last else -PEN_GAIN * mask[x + 2].astype(jnp.float32)
        turned = [None] * 3

        def add(k, change):
            turned[k] = change if turned[k] is None else turned[k] + change

        for k in range(3):
            plane = velocity[k, x + 1]
            under = None if first else velocity[k, x]
            over = None if last else velocity[k, x + 2]
            y_below, y_above = along_y(plane)
            lane = k * count_x + x
            edge = edge_of(joined, lane)
            z_below, z_above = along_z(plane, edge)
            slope[0, k, x] = (0.5 * DT_STEP) * (over if first else -under if last else over - under)
            slope[1, k, x] = (0.5 * DT_STEP) * (y_above - y_below)
            slope[2, k, x] = (0.5 * DT_STEP) * (z_above - z_below)
            penal = own * plane
            if k != 0:
                change = after * over if first else -(before * under) if last else after * over - before * under
                add(3 - k, change if k == 1 else -change)
            if k != 1:
                y_below, y_above = along_y(penal)
                change = y_above - y_below
                add(2 - k, change if k == 2 else -change)
            if k != 2:
                z_below, z_above = along_z(penal, own_edge * edge)
                change = z_above - z_below
                add(1 - k, change if k == 0 else -change)
            near = within_plane(stream[k, x + 1], edge_of(joined, 4 * count_x + lane))
            if not first:
                near = near + stream[k, x]
            if not last:
                near = near + stream[k, x + 2]
            middle[k, x + 1] = near * (1.0 / 6.0)
        for k in range(3):
            curl[k, x] = 0.5 * turned[k]


def add_x_faces(velocity, mask, stream, slope, curl, middle):
    count_x = curl.shape[1]
    for rim, x, sign in ((0, 0, -1.0), (count_x + 1, count_x - 1, 1.0)):
        gain = (-0.5 * sign * PEN_GAIN) * mask[rim].astype(jnp.float32)
        for k in range(3):
            face = velocity[k, rim]
            slope[0, k, x] += (0.5 * sign * DT_STEP) * face
            if k == 1:
                curl[2, x] += gain * face
            if k == 2:
                curl[1, x] -= gain * face
            middle[k, x + 1] += stream[k, rim] * (1.0 / 6.0)


def deposited(total, k, x, count_x, half):
    window = half + 4
    rows = pl.ds(k * window * count_x + x, window, count_x)
    count_z = total.shape[2]
    lower, upper = total[0, rows, :], total[1, rows, :]
    shared = jnp.concatenate([lower[half:], jnp.zeros((half - 4, count_z), jnp.float32)], axis=0)
    return jnp.concatenate([lower[:half], upper[:half] + shared], axis=0)


def swirl(total, slope, curl, middle, x):
    _, count_x, count_y, _ = curl.shape
    moved = [deposited(total, k, x, count_x, count_y // 2) for k in range(3)]
    for k in range(3):
        stretch = moved[0] * slope[0, k, x] + moved[1] * slope[1, k, x] + moved[2] * slope[2, k, x]
        value = moved[k] + stretch + curl[k, x]
        curl[k, x] = value
        middle[k, x + 1] += value * (1.0 / 6.0)


def within_plane(plane, edge):
    y_below, y_above = along_y(plane)
    z_below, z_above = along_z(plane, edge)
    return y_below + y_above + z_below + z_above


def second_sweep(middle, vorticity, result):
    _, count_x, count_y, count_z = vorticity.shape
    empty = jnp.zeros((count_y, count_z), jnp.float32)
    for k in range(3):
        for x in range(count_x):
            summed = within_plane(middle[k, x + 1], empty)
            if x > 0:
                summed = summed + middle[k, x]
            if x < count_x - 1:
                summed = summed + middle[k, x + 2]
            result[k, x] = (summed + vorticity[k, x]) * (1.0 / 6.0)


def pack_stream(stream, out):
    count_x = stream.shape[1] - 2
    out[...] = pack_edges([stream[k, x] for k in range(3) for x in range(1, count_x + 1)])


def step(
    strength_in, fraction_in, cell_in, target_in, velocity_in, mask_in, stream_in,
    vorticity, result, x_rim, m_in,
    strength, fraction, cell, target, velocity, mask, stream,
    outgoing, arrived, total, middle, slope, z_out, z_in, m_out,
    fetch_sem, send_sem, recv_sem, face_send, face_recv, z_send, z_recv, mx_send, mx_recv, mz_send, mz_recv,
):
    groups, patches = lax.axis_size("grp"), lax.axis_size("patch")
    g, p = lax.axis_index("grp"), lax.axis_index("patch")
    shape = vorticity.shape[1:]
    count_x = shape[0]
    fetches = [
        (strength_in, strength), (fraction_in, fraction), (cell_in, cell), (target_in, target),
        (velocity_in, velocity.at[:, pl.ds(1, count_x)]),
        (mask_in, mask.at[pl.ds(1, count_x)]),
        (stream_in, stream.at[:, pl.ds(1, count_x)]),
    ]
    fetches = [pltpu.make_async_copy(a, b, fetch_sem.at[i]) for i, (a, b) in enumerate(fetches)]
    for fetch in fetches:
        fetch.start()

    barrier = pltpu.get_barrier_semaphore()

    def greet(i, carry):
        pl.semaphore_signal(barrier, inc=1, device_id={"patch": lax.rem(p + i, patches)}, device_id_type=MESH)
        return carry

    lax.fori_loop(1, patches, greet, 0)
    sides = (
        (0, "patch", p, p > 0, p - 1), (1, "patch", p, p < patches - 1, p + 1),
        (0, "grp", g, g > 0, g - 1), (1, "grp", g, g < groups - 1, g + 1),
    )
    x_sides = [(side, there, {axis: who}) for side, axis, _, there, who in sides[:2]]
    z_sides = [(side, there, {axis: who}) for side, axis, _, there, who in sides[2:]]
    for side, there, who in z_sides:
        @pl.when(there)
        def _():
            pl.semaphore_signal(barrier, inc=1, device_id=who, device_id_type=MESH)

    for side, there, who in x_sides:
        @pl.when(jnp.logical_not(there))
        def _():
            rim = side * (count_x + 1)
            empty = jnp.zeros(velocity.shape[2:], jnp.float32)
            mask[rim] = jnp.zeros(velocity.shape[2:], jnp.int32)
            for k in range(3):
                velocity[k, rim] = empty
                stream[k, rim] = empty
                x_rim[side, k] = empty
    for side, there, who in z_sides:
        @pl.when(jnp.logical_not(there))
        def _():
            z_in[side] = jnp.zeros(z_in.shape[1:], jnp.float32)
            m_in[side] = jnp.zeros(m_in.shape[1:], jnp.float32)
    total[...] = jnp.zeros_like(total)
    for fetch in fetches[:4]:
        fetch.wait()

    def remote(a, b, send, recv, who):
        return pltpu.make_async_remote_copy(
            src_ref=a, dst_ref=b, send_sem=send, recv_sem=recv, device_id=who, device_id_type=MESH
        )

    def faces(side, who):
        own, rim = 1 + side * (count_x - 1), (1 - side) * (count_x + 1)
        return [
            remote(a, b, face_send.at[side, i], face_recv.at[1 - side, i], who)
            for i, (a, b) in enumerate((
                (velocity.at[:, own], velocity.at[:, rim]),
                (mask.at[own], mask.at[rim]),
                (stream.at[:, own], stream.at[:, rim]),
            ))
        ]

    def z_face(side, who):
        return [remote(z_out, z_in.at[1 - side], z_send.at[side], z_recv.at[1 - side], who)]

    def m_face(side, who):
        own = 1 + side * (count_x - 1)
        return [remote(middle.at[:, own], x_rim.at[1 - side], mx_send.at[side], mx_recv.at[1 - side], who)]

    def mz_face(side, who):
        return [remote(m_out, m_in.at[1 - side], mz_send.at[side], mz_recv.at[1 - side], who)]

    def start(make, ways):
        for side, there, who in ways:
            @pl.when(there)
            def _():
                for copy in make(side, who):
                    copy.start()

    def finish(make, ways, sent):
        for side, there, who in ways:
            @pl.when(there)
            def _():
                for copy in make(side if sent else 1 - side, who):
                    if sent:
                        copy.wait_send()
                    else:
                        copy.wait_recv()

    def send_faces():
        pl.semaphore_wait(barrier, patches - 1 + (g > 0).astype(jnp.int32) + (g < groups - 1).astype(jnp.int32))

    route(strength, fraction, cell, target, outgoing, lambda: None)
    late = p >= patches - patches // 4

    def pack():
        for fetch in fetches[4:]:
            fetch.wait()
        pack_faces(velocity, mask, stream, z_out)

    pl.when(jnp.logical_not(late))(pack)
    send_faces()

    def peer(i):
        return i + (i >= p).astype(jnp.int32)

    def going(i):
        other = peer(i)
        return remote(outgoing.at[other, pl.ds(0, 7)], arrived.at[p, pl.ds(0, 7)], send_sem.at[i], recv_sem.at[p], {"patch": other})

    def coming(i):
        other = peer(i)
        return remote(outgoing.at[other, pl.ds(0, 7)], arrived.at[other, pl.ds(0, 7)], send_sem.at[i], recv_sem.at[other], {"patch": other})

    def send(i, carry):
        going(i).start()
        return carry

    lax.fori_loop(0, patches - 1, send, 0)
    pl.when(late)(pack)
    start(z_face, z_sides)
    start(faces, x_sides)
    deposit([outgoing[p]], total, shape)

    def take_some(first, count):
        for i in range(count):
            coming(first + i).wait_recv()
        deposit([arrived[peer(first + i)] for i in range(count)], total, shape)

    def take(i, carry):
        take_some(i * GROUP, GROUP)
        return carry

    finish(z_face, z_sides, False)
    prepare(velocity, mask, stream, z_in, slope, vorticity, middle)
    groups_of, rest = (patches - 1) // GROUP, (patches - 1) % GROUP
    lax.fori_loop(0, groups_of, take, 0)
    if rest:
        take_some(groups_of * GROUP, rest)
    finish(faces, x_sides, False)
    add_x_faces(velocity, mask, stream, slope, vorticity, middle)
    for x in (0, count_x - 1):
        swirl(total, slope, vorticity, middle, x)
    start(m_face, x_sides)
    for x in range(1, count_x - 1):
        swirl(total, slope, vorticity, middle, x)
    pack_stream(middle, m_out)
    start(mz_face, z_sides)
    second_sweep(middle, vorticity, result)

    def sent(i, carry):
        going(i).wait_send()
        return carry

    lax.fori_loop(0, patches - 1, sent, 0)
    finish(faces, x_sides, True)
    finish(z_face, z_sides, True)
    finish(m_face, x_sides, True)
    finish(mz_face, z_sides, True)
    finish(m_face, x_sides, False)
    finish(mz_face, z_sides, False)


GROUP = 7


def write_out(vorticity, inner, x_rim, m_in, vorticity_out, result_out, result, sem):
    _, count_x, count_y, count_z = inner.shape
    written = pltpu.make_async_copy(vorticity, vorticity_out, sem.at[0])
    written.start()
    copies = [written]
    at = iota((count_y, count_z), 1)
    rim = (at == 0) | (at == count_z - 1)
    joined = join_edges(m_in[0], m_in[1])
    for k in range(3):
        for x in range(count_x):
            extra = jnp.where(rim, edge_of(joined, k * count_x + x), 0.0)
            if x == 0:
                extra = extra + x_rim[0, k]
            if x == count_x - 1:
                extra = extra + x_rim[1, k]
            result[k, x] = inner[k, x] + extra * (1.0 / 6.0)
            if x in (count_x // 2 - 1, count_x - 1):
                part = x // (count_x // 2)
                at_x = pl.ds(part * (count_x // 2), count_x // 2)
                solved = pltpu.make_async_copy(result.at[k, at_x], result_out.at[k, at_x], sem.at[1 + 2 * k + part])
                solved.start()
                copies.append(solved)
    for copy in copies:
        copy.wait()


def shards(strength, fraction, cell, patch_of, velocity, body_mask, stream_prev):
    rows = patch_of.shape[0]
    patches = lax.axis_size("patch")
    capacity = 2 * rows // patches
    parts, count_x, count_y, count_z = velocity.shape
    plane = (count_y, count_z)
    room = lambda *shape: pltpu.VMEM(shape, jnp.float32)
    ints = lambda *shape: pltpu.VMEM(shape, jnp.int32)
    dma = lambda *shape: pltpu.SemaphoreType.DMA(shape)
    whole = velocity.shape
    taken = (strength, fraction, cell.reshape(1, rows), patch_of.reshape(1, rows), velocity, body_mask, stream_prev)
    made = pl.pallas_call(
        step,
        out_shape=[room(*whole), room(*whole), room(2, parts, *plane), room(2, *plane)],
        in_specs=[HBM] * 7,
        out_specs=[VMEM] * 4,
        scratch_shapes=[
            room(3, rows), room(3, rows), ints(1, rows), ints(1, rows),
            room(parts, count_x + 2, *plane), ints(count_x + 2, *plane), room(parts, count_x + 2, *plane),
            room(patches, ROWS, capacity), room(patches, ROWS, capacity),
            room(2, parts * count_x * (count_y // 2 + 4), count_z), room(parts, count_x + 2, *plane),
            room(3, *whole),
            room(*plane), room(2, *plane), room(*plane),
            dma(7), dma(patches), dma(patches), dma(2, 3), dma(2, 3),
            dma(2), dma(2), dma(2), dma(2), dma(2), dma(2),
        ],
        compiler_params=pltpu.CompilerParams(
            collective_id=0, has_side_effects=True, vmem_limit_bytes=50 * 2**20
        ),
    )(*[pltpu.with_memory_space_constraint(array, pltpu.HBM) for array in taken])
    return tuple(pl.pallas_call(
        write_out,
        out_shape=[jax.ShapeDtypeStruct(whole, jnp.float32)] * 2,
        in_specs=[VMEM] * 4,
        out_specs=[HBM] * 2,
        scratch_shapes=[room(*whole), dma(7)],
    )(*[pltpu.with_memory_space_constraint(array, pltpu.VMEM) for array in made]))


def solution(mesh):
    in_specs = (
        P(None, ("grp", "patch")),
        P(None, ("grp", "patch")),
        P(("grp", "patch")),
        P(("grp", "patch"), None),
        P(None, "patch", None, "grp"),
        P("patch", None, "grp"),
        P(None, "patch", None, "grp"),
    )
    out_specs = (P(None, "patch", None, "grp"), P(None, "patch", None, "grp"))
    return jax.shard_map(shards, mesh=mesh, in_specs=in_specs, out_specs=out_specs, check_vma=False)
```
